128 devices in a mesh: grp: 4 (over z), req: 32 (over x, y, core).
Axes of the slice: x: 4, y: 4, z: 4, core: 2. Of those that a mesh axis runs over, the one named last changes fastest.
Arguments:
- tokens: bfloat16 [4, 8192, 1024], P('grp', 'req'), may hold values from -6 to 6
- attn_gain: float32 [1024], replicated, may hold values from 0.5 to 1.5
- w_query: bfloat16 [1024, 1024], replicated, may hold values from -0.75 to 0.75
- w_key: bfloat16 [1024, 512], replicated, may hold values from -0.75 to 0.75
- w_value: bfloat16 [1024, 512], replicated, may hold values from -0.1875 to 0.1875
- w_out: bfloat16 [1024, 1024], replicated, may hold values from -0.1875 to 0.1875
- prefix_keys: bfloat16 [4, 8192, 512], P('grp', 'req'), may hold values from -1600 to 1600
- prefix_values: bfloat16 [4, 8192, 512], P('grp', 'req'), may hold values from -6 to 6
- lengths: int32 [4, 32], P('grp'), may hold values from 1 to 256, 6144 in all within a row
- assignment: int32 [4, 32], P('grp'), may hold values from 0 to 31, each once within a row
- moe_gain: float32 [1024], replicated, may hold values from 0.5 to 1.5
- expert_ids: int32 [4, 8192, 8], P('grp', 'req'), may hold values from 0 to 31, all different within a row; in each aligned block of 256 rows (0 to 255, 256 to 511, ..., all dimensions but the last counted through in order) at most 96 rows name the same one
- route_weights: float32 [4, 8192, 8], P('grp', 'req'), may hold values from 0.1 to 0.4
- w_gate: bfloat16 [32, 1024, 512], P('req'), may hold values from -0.1875 to 0.1875
- w_up: bfloat16 [32, 1024, 512], P('req'), may hold values from -0.1875 to 0.1875
- w_down: bfloat16 [32, 512, 1024], P('req'), may hold values from -0.25 to 0.25
Outputs:
- context: bfloat16 [4, 8192, 1024], P('grp', 'req')
- hidden: bfloat16 [4, 8192, 1024], P('grp', 'req')
- expert_mix: bfloat16 [4, 8192, 1024], P('grp', 'req')
The draws below stay inside these ranges and needn't reach their ends.
Inputs may be any that keep to these rules, and one draw needn't show every extreme that they name: `lengths`: each row sums to 6144, and some request of each row has exactly 256. `assignment`: each row names every request once. `expert_ids`: each token slot names 8 different experts; within the rows of one req index no expert is named more than 96 times, a bound that some block reaches.
All inputs are finite; a program needn't handle non-finite values.
Results may differ from the reference program's by a relative error of at most 0.014.
The reference program's roundings to bfloat16 on the way count: a program that leaves them out, or rounds other values in their place, can miss the bound.
Values may be sent and summed in bfloat16 or wider, within the bound.
A program may use at most 256 MiB of HBM per device.

```python
import math
import jax
import jax.numpy as jnp
import numpy as np
from jax import lax

D = 1024
H = 16
KV = 8
HD = 64
FF = 512
EXPERTS = 32
TOP = 8
TOK_DEV = 256
GROUPS = 4
REQS = 32
TOKENS_G = 8192
SUFFIX = 6144
PREFIX = 8192
CAP = 96


def draw_prefix_keys(key, part):
    base_keys = jnp.clip(jax.random.normal(key, (GROUPS, PREFIX, KV * HD), jnp.float32) * 4.0, -24.0, 24.0)
    return base_keys.astype(jnp.bfloat16)


def steps_of(key, extent, shards, smallest, largest):
    loudness, own = 1.0, jax.random.fold_in(key, 6)
    for dim, parts in shards:
        heights = jnp.exp(jax.random.uniform(jax.random.fold_in(own, dim), (parts,), jnp.float32, smallest / len(shards), largest / len(shards)))
        loudness = loudness * jnp.repeat(heights, extent[dim] // parts).reshape([-1 if axis == dim else 1 for axis in range(len(extent))])
    return loudness


def split_up(number_of, total, limit, lean):
    weights = [(1 << 20) // math.isqrt(grade ** lean) + 1 for grade in range(2, number_of + 1)]
    surplus, holding = total - limit - (number_of - 1), [1] * (number_of - 1)
    while surplus > 0:
        free = [i for i in range(number_of - 1) if holding[i] < limit]
        whole, left = sum([weights[i] for i in free]), surplus
        for i in free:
            more = min(limit - holding[i], max(1, left * weights[i] // whole), surplus)
            holding[i] = holding[i] + more
            surplus = surplus - more
    return np.array([limit] + holding)


def ragged_sizes(rng, count, total, limit, skew):
    if count == 2:
        one = jax.random.randint(rng, (), max(1, total - limit), min(limit, total - 1) + 1)
        return jnp.stack([one, total - one])
    sizes = jnp.asarray(split_up(count, total, limit, skew), jnp.int32)
    couples = (count - 1) // 2
    giver, taker = sizes[1:1 + 2 * couples:2], sizes[2:2 + 2 * couples:2]
    margin = jnp.minimum(giver - 1, limit - taker)
    moved = jax.random.randint(jax.random.fold_in(rng, 1), (couples,), 0, 1 << 20) % (margin + 1)
    sizes = sizes.at[1:1 + 2 * couples:2].set(giver - moved).at[2:2 + 2 * couples:2].set(taker + moved)
    return sizes[jax.random.permutation(jax.random.fold_in(rng, 2), count)]


def assign_block(rng, own, number, rows, amount, top, reach, skew):
    sequence = jax.random.permutation(rng, amount)
    packed, usual = shares(amount, rows * top, reach, skew, True), shares(amount, rows * top, reach, skew, False)
    places = jnp.arange(amount)

    def named(tallies, offset_by):
        used = int((tallies > 0).sum())
        fixed = max(1, used // 4)
        passed = fixed + (places - fixed + offset_by * (used - fixed)) % max(1, amount - fixed)
        return jnp.zeros((amount,), jnp.int32).at[sequence[jnp.where(places < fixed, places, passed)]].set(jnp.asarray(tallies, jnp.int32))

    tallies = jnp.where(number % 4 == 0, named(packed, number // 4), named(usual, number - number // 4 - 1))
    mixed = jax.random.permutation(jax.random.fold_in(own, 3), amount)
    donor, receiver = mixed[0:amount // 2 * 2:2], mixed[1:amount // 2 * 2:2]
    room = jnp.minimum(tallies[donor] - 1, reach - tallies[receiver]) // 2
    room = jnp.where((donor == sequence[0]) | (receiver == sequence[0]) | (tallies[receiver] == 0), 0, jnp.maximum(room, 0))
    passed = jax.random.randint(jax.random.fold_in(own, 4), (amount // 2,), 0, 1 << 20) % (room + 1)
    tallies = tallies.at[donor].add(-passed).at[receiver].add(passed)
    labels = jnp.searchsorted(jnp.cumsum(tallies), jnp.arange(rows * top), side="right").astype(jnp.int32)
    listing = labels.reshape(top, rows).T
    listing = listing[jax.random.permutation(jax.random.fold_in(own, 1), rows)]
    offset_by = jax.random.randint(jax.random.fold_in(own, 2), (rows, 1), 0, top)
    return jnp.take_along_axis(listing, (jnp.arange(top)[None, :] + offset_by) % top, axis=1)


def shares(number_of, total, most, skew, full):
    portions = [(1 << 20) // math.isqrt(rank ** skew) + 1 for rank in range(1, number_of + 1)]
    largest = most if full else min(most, max(-(-total // number_of), total * portions[0] // sum(portions)))
    least = 1 if total - largest >= number_of - 1 else 0
    given, rest = [largest] + [least] * (number_of - 1), total - largest - least * (number_of - 1)
    while rest > 0:
        free = [i for i in range(1, number_of) if given[i] < largest] or [i for i in range(1, number_of) if given[i] < most]
        mass, remaining = sum([portions[i] for i in free]), rest
        for i in free:
            extra = min(most - given[i], max(1, remaining * portions[i] // mass), rest)
            given[i] = given[i] + extra
            rest = rest - extra
    return np.array(given)


def bell_draw(own_key, dims, deviation, limit, cuts=(), kind=jnp.bfloat16):
    level = steps_of(own_key, dims, cuts, -0.22, 0.18) if cuts else 1.0
    values = jax.random.normal(own_key, dims, jnp.float32) * deviation * level
    return jnp.minimum(jnp.maximum(values, -limit), limit).astype(kind)


def setup_inputs(seed: int = 0) -> dict:
    arg_keys = jax.random.split(jax.random.key(seed), 17)
    tokens = bell_draw(arg_keys[0], (GROUPS, TOKENS_G, D), 1.0, 6.0, ((0, 4), (1, 32)))
    attn_gain = jnp.clip(1.0 + 0.1 * jax.random.normal(arg_keys[1], (D,), jnp.float32), 0.5, 1.5)
    w_query = bell_draw(arg_keys[2], (D, H * HD), (D // 16) ** -0.5, 0.75)
    w_key = bell_draw(arg_keys[3], (D, KV * HD), (D // 16) ** -0.5, 0.75)
    w_value = bell_draw(arg_keys[4], (D, KV * HD), D ** -0.5, 0.1875)
    w_out = bell_draw(arg_keys[5], (H * HD, D), (H * HD) ** -0.5, 0.1875)
    prefix_keys = draw_prefix_keys(jax.random.fold_in(arg_keys[16], 71), 0)
    prefix_values = bell_draw(arg_keys[7], (GROUPS, PREFIX, KV * HD), 1.0, 6.0, ((0, 4), (1, 32)))
    lengths = jax.vmap(lambda own: ragged_sizes(own, REQS, SUFFIX, TOK_DEV, 2))(jax.random.split(arg_keys[8], GROUPS)).reshape((GROUPS, REQS)).astype(jnp.int32)
    assignment = jax.vmap(lambda own: jax.random.permutation(own, REQS))(jax.random.split(arg_keys[9], GROUPS)).reshape((GROUPS, REQS)).astype(jnp.int32)
    moe_gain = jnp.clip(1.0 + 0.1 * jax.random.normal(arg_keys[10], (D,), jnp.float32), 0.5, 1.5)
    expert_ids_keys = jax.random.split(jax.random.fold_in(arg_keys[11], 1), GROUPS * TOKENS_G // TOK_DEV)
    expert_ids_turns = jax.random.permutation(jax.random.fold_in(arg_keys[11], 3), GROUPS * TOKENS_G // TOK_DEV)
    expert_ids = jax.vmap(lambda own, number: assign_block(jax.random.fold_in(arg_keys[11], 2), own, number, TOK_DEV, EXPERTS, TOP, CAP, 2))(expert_ids_keys, expert_ids_turns).reshape((GROUPS, TOKENS_G, TOP))
    route_weights = jnp.clip(0.1 + 0.3 * jax.random.uniform(arg_keys[12], (GROUPS, TOKENS_G, TOP), jnp.float32) ** steps_of(arg_keys[12], (GROUPS, TOKENS_G, TOP), ((0, 4), (1, 32)), -0.2, 0.2), 0.1, 0.4)
    w_gate = bell_draw(arg_keys[13], (EXPERTS, D, FF), D ** -0.5, 0.1875, ((0, 32),))
    w_up = bell_draw(arg_keys[14], (EXPERTS, D, FF), D ** -0.5, 0.1875, ((0, 32),))
    w_down = bell_draw(arg_keys[15], (EXPERTS, FF, D), FF ** -0.5, 0.25, ((0, 32),))
    return dict(tokens=tokens, attn_gain=attn_gain, w_query=w_query, w_key=w_key, w_value=w_value, w_out=w_out, prefix_keys=prefix_keys, prefix_values=prefix_values, lengths=lengths, assignment=assignment, moe_gain=moe_gain, expert_ids=expert_ids, route_weights=route_weights, w_gate=w_gate, w_up=w_up, w_down=w_down)


NORM_EPS = 1e-06
ATTN_SCALE = 0.015625
RESIDUAL_SCALE = 0.22
ROPE_BASE = 10000.0

def normalize(head_rows, gain):
    widened = head_rows.astype(jnp.float32)
    mean_square = lax.optimization_barrier(jnp.mean(widened * widened, axis=-1, keepdims=True))
    return (widened * lax.rsqrt(mean_square + NORM_EPS) * gain).astype(jnp.bfloat16)

def rotate(head_rows, positions):
    half_dim = head_rows.shape[-1] // 2
    frequency = ROPE_BASE ** (-(jnp.arange(half_dim, dtype=jnp.float32) * 2.0 / head_rows.shape[-1]))
    angles = positions[:, None] * frequency[None, :]
    cosine = jnp.cos(angles)[:, None, :]
    sine_part = jnp.sin(angles)[:, None, :]
    first_half = head_rows[..., :half_dim]
    second_half = head_rows[..., half_dim:]
    return jnp.concatenate([first_half * cosine - second_half * sine_part, second_half * cosine + first_half * sine_part], axis=-1)

def attend_block(normed, keys_pre, values_pre, suffix_len, w_query, w_key, w_value):
    tok_count = normed.shape[0]
    positions = (PREFIX + jnp.arange(tok_count, dtype=jnp.int32)).astype(jnp.float32)
    queries = jnp.dot(normed, w_query, preferred_element_type=jnp.float32).reshape(tok_count, H, HD)
    suffix_keys = jnp.dot(normed, w_key, preferred_element_type=jnp.float32).reshape(tok_count, KV, HD)
    suffix_values = jnp.dot(normed, w_value, preferred_element_type=jnp.float32).astype(jnp.bfloat16).reshape(tok_count, KV, HD)
    queries = rotate(queries, positions).astype(jnp.bfloat16)
    suffix_keys = rotate(suffix_keys, positions).astype(jnp.bfloat16)
    keys_all = jnp.concatenate([keys_pre.reshape(PREFIX, KV, HD), suffix_keys], axis=0).astype(jnp.float32)
    values_all = jnp.concatenate([values_pre.reshape(PREFIX, KV, HD), suffix_values], axis=0).astype(jnp.float32)
    grouped = queries.astype(jnp.float32).reshape(tok_count, KV, H // KV, HD)
    scores = jnp.einsum('tkgd,skd->kgts', grouped, keys_all) * ATTN_SCALE
    column = jnp.arange(PREFIX + tok_count, dtype=jnp.int32)
    row_index = jnp.arange(tok_count, dtype=jnp.int32)
    suffix_col = column - PREFIX
    visible = (column[None, :] < PREFIX) | (suffix_col[None, :] <= row_index[:, None]) & (suffix_col[None, :] < suffix_len)
    scores = jnp.where(visible[None, None], scores, -jnp.inf)
    row_max = lax.optimization_barrier(jnp.max(scores, axis=-1, keepdims=True))
    weights = jnp.exp(scores - row_max)
    row_total = lax.optimization_barrier(jnp.sum(weights, axis=-1))
    rounded = lax.optimization_barrier(weights.astype(jnp.bfloat16)).astype(jnp.float32)
    mixed_out = jnp.einsum('kgts,skd->tkgd', rounded, values_all) / jnp.transpose(row_total, (2, 0, 1))[..., None]
    return mixed_out.reshape(tok_count, H * HD).astype(jnp.bfloat16)

def slot_numbers(ids):
    chosen = ids.reshape(-1)
    hit_table = (chosen[:, None] == jnp.arange(EXPERTS, dtype=jnp.int32)[None, :]).astype(jnp.int32)
    before = jnp.cumsum(hit_table, axis=0) - hit_table
    ranked = lax.optimization_barrier(jnp.sum(before * hit_table, axis=1))
    return (chosen, ranked)

def experts_of(moe_in, ids, gains, w_gate, w_up, w_down):
    chosen, ranked = jax.vmap(slot_numbers)(ids.reshape(REQS, TOK_DEV, TOP))
    source = jnp.arange(REQS, dtype=jnp.int32)[:, None]
    column = source * CAP + ranked
    token_rows = jnp.repeat(moe_in.reshape(REQS, TOK_DEV, D), TOP, axis=1)
    buffer_rows = jnp.zeros((EXPERTS, REQS * CAP, D), jnp.bfloat16).at[chosen, column].set(token_rows)

    def one_expert(item_set):
        expert_rows, gate_weight, up_weight, down_weight = item_set
        gate_act = jnp.dot(expert_rows, gate_weight, preferred_element_type=jnp.float32)
        up_act = jnp.dot(expert_rows, up_weight, preferred_element_type=jnp.float32)
        product = (jax.nn.silu(gate_act) * up_act).astype(jnp.bfloat16)
        return jnp.dot(product, down_weight, preferred_element_type=jnp.float32).astype(jnp.bfloat16)
    produced = lax.map(one_expert, (buffer_rows, w_gate, w_up, w_down))
    picked = produced[chosen, column].astype(jnp.float32).reshape(REQS, TOK_DEV, TOP, D)
    weighted = lax.optimization_barrier(jnp.sum(picked * gains.reshape(REQS, TOK_DEV, TOP)[..., None], axis=2))
    return weighted.reshape(TOKENS_G, D).astype(jnp.bfloat16)

def reference(tokens, attn_gain, w_query, w_key, w_value, w_out, prefix_keys, prefix_values, lengths, assignment, moe_gain, expert_ids, route_weights, w_gate, w_up, w_down):

    def one_group(item_set):
        own_rows, keys_pre, values_pre, length_row, order_row, ids, gains = item_set
        normed = normalize(own_rows, attn_gain).reshape(REQS, TOK_DEV, D)
        request_ids = jnp.arange(REQS, dtype=jnp.int32)
        own_lengths = lax.optimization_barrier(jnp.sum(jnp.where(order_row[:, None] == request_ids[None, :], length_row[None, :], 0), axis=1)).astype(jnp.int32)

        def per_index(pair_set):
            block_rows, suffix_len = pair_set
            return attend_block(block_rows, keys_pre, values_pre, suffix_len, w_query, w_key, w_value)
        context = lax.map(per_index, (normed, own_lengths)).reshape(TOKENS_G, H * HD)
        projected = jnp.dot(context, w_out, preferred_element_type=jnp.float32)
        hidden = (own_rows.astype(jnp.float32) + RESIDUAL_SCALE * projected).astype(jnp.bfloat16)
        mixed_out = experts_of(normalize(hidden, moe_gain), ids, gains, w_gate, w_up, w_down)
        return (context, hidden, mixed_out)
    context, hidden, expert_mix = lax.map(one_group, (tokens, prefix_keys, prefix_values, lengths, assignment, expert_ids, route_weights))
    return (context, hidden, expert_mix)
```

```python
import functools

import jax
import jax.numpy as jnp
import numpy as np
from jax import lax
from jax.experimental import pallas as pl
from jax.experimental.pallas import tpu as pltpu
from jax.sharding import PartitionSpec as P

HD = 64
CAP = 96
PREFIX = 8192
TOK = 256
D = 1024
FF = 512
NORM_EPS = 1e-06
ATTN_SCALE = 0.015625
RESIDUAL_SCALE = 0.22
ROPE_BASE = 10000.0
LOG2E = 1.4426950408889634
VMEM_BYTES = 60000 * 1024
BF16 = jnp.bfloat16
F32 = jnp.float32

ROW_GROUPS = [[x * 8 + y * 2 + c for x in range(4) for c in range(2)] for y in range(4)]
COL_GROUPS = [[x * 8 + y * 2 + c for y in range(4)] for x in range(4) for c in range(2)]


def rope_tables():
    half = HD // 2
    freq = np.float32(ROPE_BASE) ** (-(np.arange(half, dtype=np.float32) * 2.0 / HD))
    pos = (PREFIX + np.arange(TOK)).astype(np.float32)
    angles = (pos[:, None] * freq.astype(np.float32)[None, :]).astype(np.float64)
    cos, sin = np.cos(angles), np.sin(angles)
    cos128 = np.concatenate([cos] * 4, axis=1).astype(np.float32)
    sin128 = np.concatenate([-sin, sin, -sin, sin], axis=1).astype(np.float32)
    return cos128, sin128


def pre_kernel(tok_ref, gain_ref, wq_ref, wk_ref, wv_ref, cos_ref, sin_ref, pk_ref, pv_ref, x_ref, kv_ref):
    rows = tok_ref[...].astype(F32)
    mean_square = jnp.mean(rows * rows, axis=-1, keepdims=True)
    normed = (rows * lax.rsqrt(mean_square + NORM_EPS) * gain_ref[...]).astype(BF16)
    cos, sin = cos_ref[...], sin_ref[...]
    low = (lax.broadcasted_iota(jnp.int32, (TOK, 128), 1) & 32) == 0

    def rotate(part):
        other = jnp.where(low, pltpu.roll(part, 96, 1), pltpu.roll(part, 32, 1))
        return (part * cos + other * sin).astype(BF16)

    q = jnp.dot(normed, wq_ref[...], preferred_element_type=F32)
    k = jnp.dot(normed, wk_ref[...], preferred_element_type=F32)
    v = jnp.dot(normed, wv_ref[...], preferred_element_type=F32).astype(BF16)
    for h in range(8):
        x_ref[h, :, 0:128] = rotate(q[:, 128 * h : 128 * h + 128])
    for pair in range(4):
        kr = rotate(k[:, 128 * pair : 128 * pair + 128])
        vr = v[:, 128 * pair : 128 * pair + 128]
        x_ref[2 * pair, :, 128:256] = jnp.concatenate([kr[:, 0:64], vr[:, 0:64]], axis=1)
        x_ref[2 * pair + 1, :, 128:256] = jnp.concatenate([kr[:, 64:128], vr[:, 64:128]], axis=1)
        kr = pk_ref[:, 128 * pair : 128 * pair + 128]
        vr = pv_ref[:, 128 * pair : 128 * pair + 128]
        kv_ref[2 * pair] = jnp.concatenate([kr[:, 0:64], vr[:, 0:64]], axis=1)
        kv_ref[2 * pair + 1] = jnp.concatenate([kr[:, 64:128], vr[:, 64:128]], axis=1)


def vmem_specs(n):
    return [pl.BlockSpec(memory_space=pltpu.VMEM)] * n


def params():
    return pltpu.CompilerParams(vmem_limit_bytes=VMEM_BYTES)


def attn_kernel(kt, nq, len_ref, x_ref, kv_ref, o_ref, vt_ref, s_ref):
    b = pl.program_id(0)

    @pl.when(b == 0)
    def _():
        def tr(i, c):
            ds = pl.ds(pl.multiple_of(i * 256, 256), 256)
            vt_ref[0:64, ds] = kv_ref[ds, :].T[64:128]
            vt_ref[64:80, ds] = jnp.ones((16, 256), BF16)
            return c

        lax.fori_loop(0, PREFIX // 256, tr, 0)

    qs, accs, ms = [], [], []
    for j in range(nq):
        x = x_ref[j]
        qt = (x[:, 0:128].astype(F32) * ATTN_SCALE).astype(BF16).T
        q2 = jnp.concatenate([qt[0:64], qt[64:128]], axis=1)
        q2 = jnp.concatenate([q2, jnp.zeros((64, 512), BF16)], axis=0)
        skv = x[:, 128:256]
        s = jnp.dot(skv, q2, preferred_element_type=F32)
        srow = lax.broadcasted_iota(jnp.int32, (256, 512), 0)
        tcol = lax.broadcasted_iota(jnp.int32, (256, 512), 1) & 255
        visible = (srow <= tcol) & (srow < len_ref[b * nq + j])
        s = jnp.where(visible, s * LOG2E, -jnp.inf)
        m = jnp.max(s, axis=0, keepdims=True)
        p = jnp.exp2(s - m)
        l = jnp.sum(p, axis=0, keepdims=True)
        acc = jnp.dot(skv.T[64:128], p.astype(BF16), preferred_element_type=F32)
        accs.append(jnp.concatenate([acc, jnp.broadcast_to(l, (16, 512))], axis=0))
        qs.append(q2)
        ms.append(m)
    q2 = jnp.concatenate(qs, axis=1)
    acc = jnp.concatenate(accs, axis=1)
    m = jnp.concatenate(ms, axis=1)

    def keys(i):
        return pl.ds(pl.multiple_of(i * kt, kt), kt)

    n = PREFIX // kt
    s_ref[0] = jnp.dot(kv_ref[keys(0), :], q2, preferred_element_type=F32)

    def step(i, carry):
        m, acc = carry
        for u in range(2):
            k = 2 * i + u
            s = s_ref[u]
            s_ref[1 - u] = jnp.dot(kv_ref[keys(jnp.minimum(k + 1, n - 1)), :], q2, preferred_element_type=F32)
            s = s * LOG2E
            mn = jnp.maximum(m, jnp.max(s, axis=0, keepdims=True))
            p = jnp.exp2(s - mn).astype(BF16)
            acc = acc * jnp.exp2(m - mn) + jnp.dot(vt_ref[:, keys(k)], p, preferred_element_type=F32)
            m = mn
        return m, acc

    m, acc = lax.fori_loop(0, n // 2, step, (m, acc))
    out = acc[0:64] / acc[64:65]
    for j in range(nq):
        ot = out[:, 512 * j : 512 * (j + 1)].T.astype(BF16)
        o_ref[j] = jnp.concatenate([ot[0:256], ot[256:512]], axis=1)


def attention(lens, x, kv, kt=512, nq=2):
    return pl.pallas_call(
        functools.partial(attn_kernel, kt, nq),
        grid=(8 // nq,),
        out_shape=jax.ShapeDtypeStruct((8, TOK, 128), BF16),
        in_specs=[
            pl.BlockSpec(memory_space=pltpu.SMEM),
            pl.BlockSpec((nq, TOK, 256), lambda b: (b, 0, 0)),
            pl.BlockSpec((PREFIX, 128), lambda b: (0, 0), pipeline_mode=pl.Buffered(1)),
        ],
        out_specs=pl.BlockSpec((nq, TOK, 128), lambda b: (b, 0, 0)),
        scratch_shapes=[pltpu.VMEM((80, PREFIX), BF16), pltpu.VMEM((2, kt, 512 * nq), F32)],
        compiler_params=params(),
        cost_estimate=pl.CostEstimate(flops=60_000_000_000, bytes_accessed=4_000_000, transcendentals=35_000_000),
        name="attn",
    )(lens, x, kv)


def mid_kernel(tok_ref, ctx_ref, wo_ref, gain_ref, context_ref, hidden_ref, moe_ref):
    ctx = jnp.concatenate([ctx_ref[h] for h in range(8)], axis=1)
    context_ref[...] = ctx
    projected = jnp.dot(ctx, wo_ref[...], preferred_element_type=F32)
    hidden = (tok_ref[...].astype(F32) + RESIDUAL_SCALE * projected).astype(BF16)
    hidden_ref[...] = hidden
    wide = hidden.astype(F32)
    mean_square = jnp.mean(wide * wide, axis=-1, keepdims=True)
    moe_ref[...] = (wide * lax.rsqrt(mean_square + NORM_EPS) * gain_ref[...]).astype(BF16)


def moe_kernel(base_ref, x_ref, ids_ref, rw_ref, wg_ref, wu_ref, wd_ref, o_ref, rows_ref, eo_ref, pw_ref):
    e = pl.program_id(0)
    expert = base_ref[0] + e * 2
    tri = (
        lax.broadcasted_iota(jnp.int32, (TOK, TOK), 0) < lax.broadcasted_iota(jnp.int32, (TOK, TOK), 1)
    ).astype(BF16)
    slot = lax.broadcasted_iota(jnp.int32, (CAP, TOK), 0)
    here = pl.ds(pl.multiple_of(e * CAP, CAP), CAP)

    for b in range(8):
        hits = ids_ref[b] == expert
        mask = jnp.max(hits.astype(F32), axis=0, keepdims=True)
        weight = jnp.sum(jnp.where(hits, rw_ref[b], 0.0), axis=0, keepdims=True)
        rank = jnp.dot(jnp.broadcast_to(mask, (16, TOK)).astype(BF16), tri, preferred_element_type=F32)[0:1]
        rank = jnp.where(mask > 0, rank, -1.0).astype(jnp.int32)
        chosen = slot == rank
        rows_ref[b * CAP : (b + 1) * CAP] = jnp.dot(
            chosen.astype(BF16), x_ref[b], preferred_element_type=F32
        ).astype(BF16)
        pw_ref[b, here] = jnp.where(chosen, weight, 0.0).astype(BF16)
    rows = rows_ref[...]
    gate = jnp.dot(rows, wg_ref[0], preferred_element_type=F32)
    up = jnp.dot(rows, wu_ref[0], preferred_element_type=F32)
    act = (jax.nn.silu(gate) * up).astype(BF16)
    out = jnp.dot(act, wd_ref[0], preferred_element_type=F32).astype(BF16)
    for b in range(8):
        eo_ref[b, here] = out[b * CAP : (b + 1) * CAP]

    @pl.when(e == 3)
    def _():
        for b in range(8):
            o_ref[b] = lax.dot_general(
                pw_ref[b], eo_ref[b], (((0,), (0,)), ((), ())), preferred_element_type=F32
            ).astype(BF16)


def moe(base, x, ids, rw, wg, wu, wd):
    whole = lambda shape: pl.BlockSpec(shape, lambda e: (0,) * len(shape), pipeline_mode=pl.Buffered(1))
    return pl.pallas_call(
        moe_kernel,
        grid=(4,),
        out_shape=jax.ShapeDtypeStruct((8, TOK, D), BF16),
        in_specs=[
            pl.BlockSpec(memory_space=pltpu.SMEM),
            whole((8, TOK, D)),
            whole((8, 8, TOK)),
            whole((8, 8, TOK)),
            pl.BlockSpec((1, D, FF), lambda e: (e, 0, 0)),
            pl.BlockSpec((1, D, FF), lambda e: (e, 0, 0)),
            pl.BlockSpec((1, FF, D), lambda e: (e, 0, 0)),
        ],
        out_specs=whole((8, TOK, D)),
        scratch_shapes=[
            pltpu.VMEM((8 * CAP, D), BF16),
            pltpu.VMEM((8, 4 * CAP, D), BF16),
            pltpu.VMEM((8, 4 * CAP, TOK), BF16),
        ],
        compiler_params=params(),
        name="moe",
    )(base, x, ids, rw, wg, wu, wd)


def local(
    tokens, attn_gain, w_query, w_key, w_value, w_out, prefix_keys, prefix_values,
    lengths, assignment, moe_gain, expert_ids, route_weights, w_gate, w_up, w_down,
):
    me = lax.axis_index("req")
    x_pos, y_pos, core = me // 8, (me // 2) % 4, me % 2
    wg = lax.all_gather(w_gate, "req", axis_index_groups=COL_GROUPS, axis=0, tiled=True)
    wu = lax.all_gather(w_up, "req", axis_index_groups=COL_GROUPS, axis=0, tiled=True)
    wd = lax.all_gather(w_down, "req", axis_index_groups=COL_GROUPS, axis=0, tiled=True)
    ids = lax.all_gather(expert_ids[0].T[None], "req", axis_index_groups=ROW_GROUPS, axis=0, tiled=True)
    rw = lax.all_gather(route_weights[0].T[None], "req", axis_index_groups=ROW_GROUPS, axis=0, tiled=True)

    cos, sin = rope_tables()
    x_send, kv8 = pl.pallas_call(
        pre_kernel,
        out_shape=(
            jax.ShapeDtypeStruct((8, TOK, 256), BF16),
            jax.ShapeDtypeStruct((8, TOK, 128), BF16),
        ),
        in_specs=vmem_specs(9),
        out_specs=tuple(vmem_specs(2)),
        compiler_params=params(),
        name="pre",
    )(tokens[0], attn_gain[None], w_query, w_key, w_value, cos, sin, prefix_keys[0], prefix_values[0])
    kv_send = jnp.broadcast_to(kv8.reshape(4, 1, 2, TOK, 128), (4, 4, 2, TOK, 128)).reshape(32, TOK, 128)
    kv = lax.all_to_all(kv_send, "req", split_axis=0, concat_axis=0, tiled=True).reshape(PREFIX, 128)
    x = lax.all_to_all(x_send, "req", split_axis=0, concat_axis=0, tiled=True, axis_index_groups=ROW_GROUPS)

    row = jnp.arange(8, dtype=jnp.int32)
    members = (row // 2) * 8 + y_pos * 2 + row % 2
    numbers = jnp.arange(32, dtype=jnp.int32)
    request = jnp.sum(jnp.where(members[:, None] == numbers[None, :], assignment[0][None, :], 0), axis=1)
    lens = jnp.sum(jnp.where(request[:, None] == numbers[None, :], lengths[0][None, :], 0), axis=1)

    part = attention(lens, x, kv)
    ctx = lax.all_to_all(part, "req", split_axis=0, concat_axis=0, tiled=True, axis_index_groups=ROW_GROUPS)
    context, hidden, moe_in = pl.pallas_call(
        mid_kernel,
        out_shape=tuple(jax.ShapeDtypeStruct((TOK, D), BF16) for _ in range(3)),
        in_specs=vmem_specs(4),
        out_specs=tuple(vmem_specs(3)),
        compiler_params=params(),
        name="mid",
    )(tokens[0], ctx, w_out, moe_gain[None])
    moe_all = lax.all_gather(moe_in[None], "req", axis_index_groups=ROW_GROUPS, axis=0, tiled=True)
    base = (x_pos * 8 + core).reshape(1).astype(jnp.int32)
    mixed = moe(base, moe_all, ids, rw, wg, wu, wd)
    expert_mix = lax.psum_scatter(
        mixed, "req", scatter_dimension=0, axis_index_groups=ROW_GROUPS, tiled=True
    )
    return (context[None], hidden[None], expert_mix)


def solution(mesh):
    placed = (
        P("grp", "req", None), P(), P(), P(), P(), P(),
        P("grp", "req", None), P("grp", "req", None), P("grp", None), P("grp", None),
        P(), P("grp", "req", None), P("grp", "req", None),
        P("req", None, None), P("req", None, None), P("req", None, None),
    )
    return jax.shard_map(
        local,
        mesh=mesh,
        in_specs=placed,
        out_specs=(P("grp", "req", None), P("grp", "req", None), P("grp", "req", None)),
        check_vma=False,
    )
```

```python
import functools

import jax
import jax.numpy as jnp
import numpy as np
from jax import lax
from jax.experimental import pallas as pl
from jax.experimental.pallas import tpu as pltpu
from jax.sharding import PartitionSpec as P

HD = 64
CAP = 96
PREFIX = 8192
TOK = 256
D = 1024
FF = 512
NORM_EPS = 1e-06
ATTN_SCALE = 0.015625
RESIDUAL_SCALE = 0.22
ROPE_BASE = 10000.0
LOG2E = 1.4426950408889634
VMEM_BYTES = 60000 * 1024
BF16 = jnp.bfloat16
F32 = jnp.float32

ROW_GROUPS = [[x * 8 + y * 2 + c for x in range(4) for c in range(2)] for y in range(4)]


def rope_tables():
    half = HD // 2
    freq = np.float32(ROPE_BASE) ** (-(np.arange(half, dtype=np.float32) * 2.0 / HD))
    pos = (PREFIX + np.arange(TOK)).astype(np.float32)
    angles = (pos[:, None] * freq.astype(np.float32)[None, :]).astype(np.float64)
    cos, sin = np.cos(angles), np.sin(angles)
    cos128 = np.concatenate([cos] * 4, axis=1).astype(np.float32)
    sin128 = np.concatenate([-sin, sin, -sin, sin], axis=1).astype(np.float32)
    return cos128, sin128


def vmem_specs(n):
    return [pl.BlockSpec(memory_space=pltpu.VMEM)] * n


def params():
    return pltpu.CompilerParams(vmem_limit_bytes=VMEM_BYTES)


MESH_ID = pl.DeviceIdType.MESH
KT = 512
ORDER = (0, 1, 3, 2)
WIDE = ((512, 128), (512, 128), (256, 64))


def rem4(v):
    return lax.rem(v + 4, 4)


def front_kernel(
    tok_ref, again_ref, wq_ref, wk_ref, wv_ref, wo_ref, mgain_ref, cos_ref, sin_ref, pk_ref, pv_ref, len_ref,
    ids_in, rw_in, g_in, u_in, d_in,
    context_ref, hidden_ref, moe_all, ids_all, rw_all, g_all, u_all, d_all,
    kv8, kv_all, x_send, x_all, vt_ref, s_ref, part_ref, ctx_all, moe_buf,
    kvs, kvr, xs, xr, cs, cr, ms, mr, ts, tr, ws, wr, vs, vr, zs, zr, own_sem,
):
    grp = lax.axis_index("grp")
    me = lax.axis_index("req")
    x, y, c = lax.div(me, 8), lax.rem(lax.div(me, 2), 4), lax.rem(me, 2)
    pos = 2 * x + c

    def remote(src, dst, send, recv, tx, ty, tc, tg=None):
        where = (grp if tg is None else tg, tx * 8 + ty * 2 + tc)
        return pltpu.make_async_remote_copy(
            src_ref=src, dst_ref=dst, send_sem=send, recv_sem=recv, device_id=where, device_id_type=MESH_ID
        )

    barrier = pltpu.get_barrier_semaphore()

    def greet(i, carry):
        pl.semaphore_signal(barrier, inc=1, device_id=(grp, lax.rem(me + i, 32)), device_id_type=MESH_ID)
        return carry

    lax.fori_loop(1, 32, greet, 0)
    for dz in (1, 2, 3):
        pl.semaphore_signal(barrier, inc=1, device_id=(rem4(grp + dz), me), device_id_type=MESH_ID)

    def own_copies():
        pairs = [(g_in.at[0], g_all.at[3]), (u_in.at[0], u_all.at[3]), (d_in.at[0], d_all.at[3]),
                 (ids_in, ids_all.at[pos]), (rw_in, rw_all.at[pos])]
        return [pltpu.make_async_copy(a, b, own_sem.at[i]) for i, (a, b) in enumerate(pairs)]

    for cp in own_copies():
        cp.start()

    for pair in range(4):
        kr = pk_ref[:, 128 * pair : 128 * pair + 128]
        vr_ = pv_ref[:, 128 * pair : 128 * pair + 128]
        kv8[2 * pair] = jnp.concatenate([kr[:, 0:64], vr_[:, 0:64]], axis=1)
        kv8[2 * pair + 1] = jnp.concatenate([kr[:, 64:128], vr_[:, 64:128]], axis=1)
    mine = pl.ds(pl.multiple_of(me * TOK, TOK), TOK)
    kv_all[mine, :] = kv8[pos]
    pl.semaphore_wait(barrier, 34)

    def kv_copy(j, tc):
        tx, ty = lax.rem(x + lax.div(j, 4), 4), lax.rem(y + lax.rem(j, 4), 4)
        return remote(kv8.at[2 * tx + tc], kv_all.at[mine, :], kvs.at[2 * j + tc], kvr.at[me], tx, ty, tc)

    def kv_send(j, carry):
        for tc in (0, 1):
            kv_copy(j, tc).start()
        return carry

    kv_copy(0, 1 - c).start()
    lax.fori_loop(1, 16, kv_send, 0)

    peers = [(0, 1)] + [(dx, dc) for dx in (1, 3, 2) for dc in (0, 1)]

    def peer(i):
        dx, dc = peers[i]
        return rem4(x + dx), lax.rem(c + dc, 2)

    def table_copies(i):
        tx, tc = peer(i)
        return (
            remote(ids_in, ids_all.at[pos], ts.at[0, i], tr.at[0, i], tx, y, tc),
            remote(rw_in, rw_all.at[pos], ts.at[1, i], tr.at[1, i], tx, y, tc),
        )

    for i in range(7):
        for cp in table_copies(i):
            cp.start()

    stacks = ((g_in, g_all), (u_in, u_all), (d_in, d_all))

    def quarter_rows(t):
        straight, quarter = WIDE[t]
        return pl.ds(pl.multiple_of(straight + grp * quarter, 16), quarter)

    def weight_copies(dy, part):
        out = []
        for t, (src, dst) in enumerate(stacks):
            rows = quarter_rows(t) if part else pl.ds(0, WIDE[t][0])
            sems = (vs, vr) if part else (ws, wr)
            out.append(
                remote(src.at[0, rows, :], dst.at[3 - dy, rows, :], sems[0].at[dy - 1, t], sems[1].at[dy - 1, t],
                       x, rem4(y + dy), c)
            )
        return out

    def column_copies(dz, slot):
        out = []
        for t, (src, dst) in enumerate(stacks):
            rows = quarter_rows(t)
            out.append(
                remote(dst.at[slot, rows, :], dst.at[slot, rows, :], zs.at[dz - 1, slot, t], zr.at[dz - 1, slot, t],
                       x, y, c, rem4(grp + dz))
            )
        return out

    for part in (1, 0):
        for dy in (1, 3, 2):
            for cp in weight_copies(dy, part):
                cp.start()

    rows = tok_ref[...].astype(F32)
    mean_square = jnp.mean(rows * rows, axis=-1, keepdims=True)
    normed = (rows * lax.rsqrt(mean_square + NORM_EPS) * again_ref[...]).astype(BF16)
    cos, sin = cos_ref[...], sin_ref[...]
    low = (lax.broadcasted_iota(jnp.int32, (TOK, 128), 1) & 32) == 0

    def rotate(part):
        other = jnp.where(low, pltpu.roll(part, 96, 1), pltpu.roll(part, 32, 1))
        return (part * cos + other * sin).astype(BF16)

    q = jnp.dot(normed, wq_ref[...], preferred_element_type=F32)
    k = jnp.dot(normed, wk_ref[...], preferred_element_type=F32)
    v = jnp.dot(normed, wv_ref[...], preferred_element_type=F32).astype(BF16)
    for h in range(8):
        x_send[h, :, 0:128] = rotate(q[:, 128 * h : 128 * h + 128])
    for pair in range(4):
        kr = rotate(k[:, 128 * pair : 128 * pair + 128])
        vr_ = v[:, 128 * pair : 128 * pair + 128]
        x_send[2 * pair, :, 128:256] = jnp.concatenate([kr[:, 0:64], vr_[:, 0:64]], axis=1)
        x_send[2 * pair + 1, :, 128:256] = jnp.concatenate([kr[:, 64:128], vr_[:, 64:128]], axis=1)
    x_all[pos] = x_send[pos]

    def x_copy(i):
        tx, tc = peer(i)
        return remote(x_send.at[2 * tx + tc], x_all.at[pos], xs.at[i], xr.at[i], tx, y, tc)

    for i in range(7):
        x_copy(i).start()

    vt_ref[64:80, :] = jnp.ones((16, PREFIX), BF16)

    def keys_of(first, j):
        if first:
            sx, sy = lax.rem(x + 4 - lax.div(j, 4), 4), lax.rem(y + 4 - lax.rem(j, 4), 4)
            chip = sx * 4 + sy
        else:
            chip = j
        return chip, pl.ds(pl.multiple_of(chip * KT, KT), KT)

    def arrive(src):
        spot = pl.ds(pl.multiple_of(src * TOK, TOK), TOK)
        remote(kv8.at[0], kv_all.at[spot, :], kvs.at[0], kvr.at[src], x, y, 1 - c).wait_recv()

    def score(first, j, q2):
        chip, ds = keys_of(first, j)
        block = kv_all[ds, :]
        if first:
            vt_ref[0:64, ds] = block.T[64:128]
        return jnp.dot(block, q2, preferred_element_type=F32)

    def attend(kth):
        first = kth == 0
        tx = rem4(x + ORDER[kth])
        back = (4 - ORDER[kth]) % 4
        for i, (dx, dc) in enumerate(peers):
            if dx == back:
                x_copy(i).wait_recv()
        qs, accs, maxes = [], [], []
        for j in range(2):
            blk = x_all[2 * tx + j]
            qt = (blk[:, 0:128].astype(F32) * ATTN_SCALE).astype(BF16).T
            q2 = jnp.concatenate([qt[0:64], qt[64:128]], axis=1)
            q2 = jnp.concatenate([q2, jnp.zeros((64, 512), BF16)], axis=0)
            skv = blk[:, 128:256]
            s = jnp.dot(skv, q2, preferred_element_type=F32)
            srow = lax.broadcasted_iota(jnp.int32, (TOK, 512), 0)
            tcol = lax.broadcasted_iota(jnp.int32, (TOK, 512), 1) & 255
            visible = (srow <= tcol) & (srow < len_ref[2 * tx + j])
            s = jnp.where(visible, s * LOG2E, -jnp.inf)
            m = jnp.max(s, axis=0, keepdims=True)
            p = jnp.exp2(s - m)
            l = jnp.sum(p, axis=0, keepdims=True)
            acc = jnp.dot(skv.T[64:128], p.astype(BF16), preferred_element_type=F32)
            accs.append(jnp.concatenate([acc, jnp.broadcast_to(l, (16, 512))], axis=0))
            qs.append(q2)
            maxes.append(m)
        q2 = jnp.concatenate(qs, axis=1)
        acc = jnp.concatenate(accs, axis=1)
        m = jnp.concatenate(maxes, axis=1)
        n = PREFIX // KT
        if first:
            arrive(2 * (4 * x + y) + 1 - c)
        s_ref[0] = score(first, jnp.int32(0), q2)

        def step(i, carry):
            m, acc = carry
            for u in range(2):
                kk = 2 * i + u
                nxt = jnp.minimum(kk + 1, n - 1)
                if first:

                    @pl.when(kk + 1 < n)
                    def _():
                        chip, ds = keys_of(first, nxt)
                        arrive(2 * chip)
                        arrive(2 * chip + 1)

                s = s_ref[u]
                s_ref[1 - u] = score(first, nxt, q2)
                s = s * LOG2E
                mn = jnp.maximum(m, jnp.max(s, axis=0, keepdims=True))
                p = jnp.exp2(s - mn).astype(BF16)
                chip, ds = keys_of(first, kk)
                acc = acc * jnp.exp2(m - mn) + jnp.dot(vt_ref[:, ds], p, preferred_element_type=F32)
                m = mn
            return m, acc

        m, acc = lax.fori_loop(0, n // 2, step, (m, acc))
        out = acc[0:64] / acc[64:65]
        for j in range(2):
            ot = out[:, 512 * j : 512 * (j + 1)].T.astype(BF16)
            part_ref[2 * tx + j] = jnp.concatenate([ot[0:256], ot[256:512]], axis=1)

    def ctx_copy(i):
        tx, tc = peer(i)
        return remote(part_ref.at[2 * tx + tc], ctx_all.at[pos], cs.at[i], cr.at[i], tx, y, tc)

    for kth in range(4):
        if kth == 2:
            for slot_dy in (1, 3, 2):
                for cp in weight_copies(slot_dy, 1):
                    cp.wait_recv()
            for slot in range(3):
                for dz in (1, 3, 2):
                    for cp in column_copies(dz, slot):
                        cp.start()
        attend(kth)
        if kth == 0:
            ctx_all[pos] = part_ref[pos]
        for i, (dx, dc) in enumerate(peers):
            if dx == ORDER[kth]:
                ctx_copy(i).start()

    for i in range(7):
        ctx_copy(i).wait_recv()
    ctx = jnp.concatenate([ctx_all[h] for h in range(8)], axis=1)
    context_ref[...] = ctx
    projected = jnp.dot(ctx, wo_ref[...], preferred_element_type=F32)
    hidden = (tok_ref[...].astype(F32) + RESIDUAL_SCALE * projected).astype(BF16)
    hidden_ref[...] = hidden
    wide = hidden.astype(F32)
    mean_square = jnp.mean(wide * wide, axis=-1, keepdims=True)
    moe_buf[...] = (wide * lax.rsqrt(mean_square + NORM_EPS) * mgain_ref[...]).astype(BF16)

    def moe_copy(i, dx):
        return remote(moe_buf, moe_all.at[pos], ms.at[i], mr.at[i], rem4(x + dx), y, c)

    def relay_copy(i, spot, src):
        return remote(src, moe_all.at[spot], ms.at[3 + i], mr.at[3 + i], x, y, 1 - c)

    keep = pltpu.make_async_copy(moe_buf, moe_all.at[pos], own_sem.at[5])
    for i, dx in enumerate((1, 3, 2)):
        moe_copy(i, dx).start()
    relay_copy(3, pos, moe_buf).start()
    keep.start()
    relays = []
    for i, dx in enumerate((1, 3, 2)):
        moe_copy(i, dx).wait_recv()
        spot = 2 * rem4(x - dx) + c
        cp = relay_copy(i, spot, moe_all.at[spot])
        cp.start()
        relays.append(cp)

    keep.wait()
    for cp in own_copies():
        cp.wait()
    for i, dx in enumerate((1, 3, 2)):
        moe_copy(i, dx).wait_send()
    for cp in relays + [relay_copy(3, pos, moe_buf)]:
        cp.wait()
    for i in range(7):
        x_copy(i).wait_send()
        ctx_copy(i).wait_send()
        for cp in table_copies(i):
            cp.wait()
    kv_copy(0, 1 - c).wait_send()

    def kv_done(j, carry):
        for tc in (0, 1):
            kv_copy(j, tc).wait_send()
        return carry

    lax.fori_loop(1, 16, kv_done, 0)
    for dy in (1, 3, 2):
        for cp in weight_copies(dy, 1):
            cp.wait_send()
        for cp in weight_copies(dy, 0):
            cp.wait()
    for slot in range(3):
        for dz in (1, 3, 2):
            for cp in column_copies(dz, slot):
                cp.wait()


def front(*args):
    anywhere = pl.BlockSpec(memory_space=pl.ANY)
    dma = pltpu.SemaphoreType.DMA
    shape = jax.ShapeDtypeStruct
    return pl.pallas_call(
        front_kernel,
        out_shape=(
            shape((TOK, D), BF16), shape((TOK, D), BF16), shape((8, TOK, D), BF16),
            shape((8, 8, TOK), jnp.int32), shape((8, 8, TOK), F32),
            shape((4, D, FF), BF16), shape((4, D, FF), BF16), shape((4, FF, D), BF16),
        ),
        in_specs=vmem_specs(12) + [anywhere] * 5,
        out_specs=tuple(vmem_specs(2) + [anywhere] * 6),
        scratch_shapes=[
            pltpu.VMEM((8, TOK, 128), BF16),
            pltpu.VMEM((PREFIX, 128), BF16),
            pltpu.VMEM((8, TOK, 256), BF16),
            pltpu.VMEM((8, TOK, 256), BF16),
            pltpu.VMEM((80, PREFIX), BF16),
            pltpu.VMEM((2, KT, 1024), F32),
            pltpu.VMEM((8, TOK, 128), BF16),
            pltpu.VMEM((8, TOK, 128), BF16),
            pltpu.VMEM((TOK, D), BF16),
            dma((32,)), dma((32,)), dma((7,)), dma((7,)), dma((7,)), dma((7,)), dma((7,)), dma((7,)),
            dma((2, 7)), dma((2, 7)), dma((3, 3)), dma((3, 3)), dma((3, 3)), dma((3, 3)),
            dma((3, 3, 3)), dma((3, 3, 3)), dma((6,)),
        ],
        compiler_params=pltpu.CompilerParams(
            vmem_limit_bytes=VMEM_BYTES, collective_id=0, has_side_effects=True
        ),
        name="front",
    )(*args)


def moe_kernel(experts_ref, x_ref, ids_ref, rw_ref, wg_ref, wu_ref, wd_ref, o_ref, rows_ref, eo_ref, pw_ref):
    e = pl.program_id(0)
    expert = experts_ref[e]
    tri = (
        lax.broadcasted_iota(jnp.int32, (TOK, TOK), 0) < lax.broadcasted_iota(jnp.int32, (TOK, TOK), 1)
    ).astype(BF16)
    slot = lax.broadcasted_iota(jnp.int32, (CAP, TOK), 0)
    here = pl.ds(pl.multiple_of(e * CAP, CAP), CAP)

    for b in range(8):
        hits = ids_ref[b] == expert
        mask = jnp.max(hits.astype(F32), axis=0, keepdims=True)
        weight = jnp.sum(jnp.where(hits, rw_ref[b], 0.0), axis=0, keepdims=True)
        rank = jnp.dot(jnp.broadcast_to(mask, (16, TOK)).astype(BF16), tri, preferred_element_type=F32)[0:1]
        rank = jnp.where(mask > 0, rank, -1.0).astype(jnp.int32)
        chosen = slot == rank
        rows_ref[b * CAP : (b + 1) * CAP] = jnp.dot(
            chosen.astype(BF16), x_ref[b], preferred_element_type=F32
        ).astype(BF16)
        pw_ref[b, here] = jnp.where(chosen, weight, 0.0).astype(BF16)
    rows = rows_ref[...]
    gate = jnp.dot(rows, wg_ref[0], preferred_element_type=F32)
    up = jnp.dot(rows, wu_ref[0], preferred_element_type=F32)
    act = (jax.nn.silu(gate) * up).astype(BF16)
    out = jnp.dot(act, wd_ref[0], preferred_element_type=F32).astype(BF16)
    for b in range(8):
        eo_ref[b, here] = out[b * CAP : (b + 1) * CAP]

    @pl.when(e == 3)
    def _():
        for b in range(8):
            o_ref[b] = lax.dot_general(
                pw_ref[b], eo_ref[b], (((0,), (0,)), ((), ())), preferred_element_type=F32
            ).astype(BF16)


def moe(experts, x, ids, rw, wg, wu, wd):
    whole = lambda shape: pl.BlockSpec(shape, lambda e: (0,) * len(shape), pipeline_mode=pl.Buffered(1))
    return pl.pallas_call(
        moe_kernel,
        grid=(4,),
        out_shape=jax.ShapeDtypeStruct((8, TOK, D), BF16),
        in_specs=[
            pl.BlockSpec(memory_space=pltpu.SMEM),
            whole((8, TOK, D)),
            whole((8, 8, TOK)),
            whole((8, 8, TOK)),
            pl.BlockSpec((1, D, FF), lambda e: (e, 0, 0)),
            pl.BlockSpec((1, D, FF), lambda e: (e, 0, 0)),
            pl.BlockSpec((1, FF, D), lambda e: (e, 0, 0)),
        ],
        out_specs=whole((8, TOK, D)),
        scratch_shapes=[
            pltpu.VMEM((8 * CAP, D), BF16),
            pltpu.VMEM((8, 4 * CAP, D), BF16),
            pltpu.VMEM((8, 4 * CAP, TOK), BF16),
        ],
        compiler_params=params(),
        name="moe",
    )(experts, x, ids, rw, wg, wu, wd)


def local(
    tokens, attn_gain, w_query, w_key, w_value, w_out, prefix_keys, prefix_values,
    lengths, assignment, moe_gain, expert_ids, route_weights, w_gate, w_up, w_down,
):
    me = lax.axis_index("req")
    x_pos, y_pos, core = me // 8, (me // 2) % 4, me % 2
    row = jnp.arange(8, dtype=jnp.int32)
    members = (row // 2) * 8 + y_pos * 2 + row % 2
    numbers = jnp.arange(32, dtype=jnp.int32)
    request = jnp.sum(jnp.where(members[:, None] == numbers[None, :], assignment[0][None, :], 0), axis=1)
    lens = jnp.sum(jnp.where(request[:, None] == numbers[None, :], lengths[0][None, :], 0), axis=1)
    lens = jnp.broadcast_to(lens[:, None, None], (8, 1, 512))
    cos, sin = rope_tables()
    context, hidden, moe_all, ids, rw, wg, wu, wd = front(
        tokens[0], attn_gain[None], w_query, w_key, w_value, w_out, moe_gain[None], cos, sin,
        prefix_keys[0], prefix_values[0], lens, expert_ids[0].T, route_weights[0].T, w_gate, w_up, w_down,
    )
    slots = jnp.arange(4, dtype=jnp.int32)
    experts = (x_pos * 8 + ((y_pos + 1 + slots) % 4) * 2 + core).astype(jnp.int32)
    mixed = moe(experts, moe_all, ids, rw, wg, wu, wd)
    expert_mix = lax.psum_scatter(
        mixed, "req", scatter_dimension=0, axis_index_groups=ROW_GROUPS, tiled=True
    )
    return (context[None], hidden[None], expert_mix)


def solution(mesh):
    placed = (
        P("grp", "req", None), P(), P(), P(), P(), P(),
        P("grp", "req", None), P("grp", "req", None), P("grp", None), P("grp", None),
        P(), P("grp", "req", None), P("grp", "req", None),
        P("req", None, None), P("req", None, None), P("req", None, None),
    )
    return jax.shard_map(
        local,
        mesh=mesh,
        in_specs=placed,
        out_specs=(P("grp", "req", None), P("grp", "req", None), P("grp", "req", None)),
        check_vma=False,
    )
```

```python
import functools

import jax
import jax.numpy as jnp
import numpy as np
from jax import lax
from jax.experimental import pallas as pl
from jax.experimental.pallas import tpu as pltpu
from jax.sharding import PartitionSpec as P

HD = 64
CAP = 96
PREFIX = 8192
TOK = 256
D = 1024
FF = 512
NORM_EPS = 1e-06
ATTN_SCALE = 0.015625
RESIDUAL_SCALE = 0.22
ROPE_BASE = 10000.0
LOG2E = 1.4426950408889634
VMEM_BYTES = 60000 * 1024
BF16 = jnp.bfloat16
F32 = jnp.float32


def rope_tables():
    half = HD // 2
    freq = np.float32(ROPE_BASE) ** (-(np.arange(half, dtype=np.float32) * 2.0 / HD))
    pos = (PREFIX + np.arange(TOK)).astype(np.float32)
    angles = (pos[:, None] * freq.astype(np.float32)[None, :]).astype(np.float64)
    cos, sin = np.cos(angles), np.sin(angles)
    cos128 = np.concatenate([cos] * 4, axis=1).astype(np.float32)
    sin128 = np.concatenate([-sin, sin, -sin, sin], axis=1).astype(np.float32)
    return cos128, sin128


def vmem_specs(n):
    return [pl.BlockSpec(memory_space=pltpu.VMEM)] * n


def params():
    return pltpu.CompilerParams(vmem_limit_bytes=VMEM_BYTES)


MESH_ID = pl.DeviceIdType.MESH
KT = 512
ORDER = (0, 1, 3, 2)
WIDE = ((512, 128), (512, 128), (256, 64))


def rem4(v):
    return lax.rem(v + 4, 4)


def front_kernel(
    tok_ref, again_ref, wq_ref, wk_ref, wv_ref, wo_ref, mgain_ref, cos_ref, sin_ref, pk_ref, pv_ref, len_ref,
    ids_in, rw_in, g_in, u_in, d_in,
    context_ref, hidden_ref, moe_all, ids_all, rw_all, g_all, u_all, d_all,
    kv8, kv_all, x_send, x_all, vt_ref, s_ref, part_ref, ctx_all, moe_buf,
    kvs, kvr, xs, xr, cs, cr, ms, mr, ts, tr, ws, wr, vs, vr, zs, zr, own_sem,
):
    grp = lax.axis_index("grp")
    me = lax.axis_index("req")
    x, y, c = lax.div(me, 8), lax.rem(lax.div(me, 2), 4), lax.rem(me, 2)
    pos = 2 * x + c

    def remote(src, dst, send, recv, tx, ty, tc, tg=None):
        where = (grp if tg is None else tg, tx * 8 + ty * 2 + tc)
        return pltpu.make_async_remote_copy(
            src_ref=src, dst_ref=dst, send_sem=send, recv_sem=recv, device_id=where, device_id_type=MESH_ID
        )

    barrier = pltpu.get_barrier_semaphore()

    def greet(i, carry):
        pl.semaphore_signal(barrier, inc=1, device_id=(grp, lax.rem(me + i, 32)), device_id_type=MESH_ID)
        return carry

    lax.fori_loop(1, 32, greet, 0)
    for dz in (1, 2, 3):
        pl.semaphore_signal(barrier, inc=1, device_id=(rem4(grp + dz), me), device_id_type=MESH_ID)

    def own_copies():
        pairs = [(g_in.at[0], g_all.at[3]), (u_in.at[0], u_all.at[3]), (d_in.at[0], d_all.at[3]),
                 (ids_in, ids_all.at[pos]), (rw_in, rw_all.at[pos])]
        return [pltpu.make_async_copy(a, b, own_sem.at[i]) for i, (a, b) in enumerate(pairs)]

    for cp in own_copies():
        cp.start()

    for pair in range(4):
        kr = pk_ref[:, 128 * pair : 128 * pair + 128]
        vr_ = pv_ref[:, 128 * pair : 128 * pair + 128]
        kv8[2 * pair] = jnp.concatenate([kr[:, 0:64], vr_[:, 0:64]], axis=1)
        kv8[2 * pair + 1] = jnp.concatenate([kr[:, 64:128], vr_[:, 64:128]], axis=1)
    mine = pl.ds(pl.multiple_of(me * TOK, TOK), TOK)
    kv_all[mine, :] = kv8[pos]
    pl.semaphore_wait(barrier, 34)

    def kv_copy(j, tc):
        tx, ty = lax.rem(x + lax.div(j, 4), 4), lax.rem(y + lax.rem(j, 4), 4)
        return remote(kv8.at[2 * tx + tc], kv_all.at[mine, :], kvs.at[2 * j + tc], kvr.at[me], tx, ty, tc)

    def kv_send(j, carry):
        for tc in (0, 1):
            kv_copy(j, tc).start()
        return carry

    kv_copy(0, 1 - c).start()
    lax.fori_loop(1, 16, kv_send, 0)

    peers = [(0, 1)] + [(dx, dc) for dx in (1, 3, 2) for dc in (0, 1)]

    def peer(i):
        dx, dc = peers[i]
        return rem4(x + dx), lax.rem(c + dc, 2)

    def table_copies(i):
        tx, tc = peer(i)
        return (
            remote(ids_in, ids_all.at[pos], ts.at[0, i], tr.at[0, i], tx, y, tc),
            remote(rw_in, rw_all.at[pos], ts.at[1, i], tr.at[1, i], tx, y, tc),
        )

    for i in range(7):
        for cp in table_copies(i):
            cp.start()

    stacks = ((g_in, g_all), (u_in, u_all), (d_in, d_all))

    def quarter_rows(t):
        straight, quarter = WIDE[t]
        return pl.ds(pl.multiple_of(straight + grp * quarter, 16), quarter)

    def weight_copies(dy, part):
        out = []
        for t, (src, dst) in enumerate(stacks):
            rows = quarter_rows(t) if part else pl.ds(0, WIDE[t][0])
            sems = (vs, vr) if part else (ws, wr)
            out.append(
                remote(src.at[0, rows, :], dst.at[3 - dy, rows, :], sems[0].at[dy - 1, t], sems[1].at[dy - 1, t],
                       x, rem4(y + dy), c)
            )
        return out

    def column_copies(dz, slot):
        out = []
        for t, (src, dst) in enumerate(stacks):
            rows = quarter_rows(t)
            out.append(
                remote(dst.at[slot, rows, :], dst.at[slot, rows, :], zs.at[dz - 1, slot, t], zr.at[dz - 1, slot, t],
                       x, y, c, rem4(grp + dz))
            )
        return out

    for part in (1, 0):
        for dy in (1, 3, 2):
            for cp in weight_copies(dy, part):
                cp.start()

    rows = tok_ref[...].astype(F32)
    mean_square = jnp.mean(rows * rows, axis=-1, keepdims=True)
    normed = (rows * lax.rsqrt(mean_square + NORM_EPS) * again_ref[...]).astype(BF16)
    cos, sin = cos_ref[...], sin_ref[...]
    low = (lax.broadcasted_iota(jnp.int32, (TOK, 128), 1) & 32) == 0

    def rotate(part):
        other = jnp.where(low, pltpu.roll(part, 96, 1), pltpu.roll(part, 32, 1))
        return (part * cos + other * sin).astype(BF16)

    q = jnp.dot(normed, wq_ref[...], preferred_element_type=F32)
    k = jnp.dot(normed, wk_ref[...], preferred_element_type=F32)
    v = jnp.dot(normed, wv_ref[...], preferred_element_type=F32).astype(BF16)
    for h in range(8):
        x_send[h, :, 0:128] = rotate(q[:, 128 * h : 128 * h + 128])
    for pair in range(4):
        kr = rotate(k[:, 128 * pair : 128 * pair + 128])
        vr_ = v[:, 128 * pair : 128 * pair + 128]
        x_send[2 * pair, :, 128:256] = jnp.concatenate([kr[:, 0:64], vr_[:, 0:64]], axis=1)
        x_send[2 * pair + 1, :, 128:256] = jnp.concatenate([kr[:, 64:128], vr_[:, 64:128]], axis=1)
    x_all[pos] = x_send[pos]

    def x_copy(i):
        tx, tc = peer(i)
        return remote(x_send.at[2 * tx + tc], x_all.at[pos], xs.at[i], xr.at[i], tx, y, tc)

    for i in range(7):
        x_copy(i).start()

    vt_ref[64:80, :] = jnp.ones((16, PREFIX), BF16)

    def keys_of(first, j):
        if first:
            sx, sy = lax.rem(x + 4 - lax.div(j, 4), 4), lax.rem(y + 4 - lax.rem(j, 4), 4)
            chip = sx * 4 + sy
        else:
            chip = j
        return chip, pl.ds(pl.multiple_of(chip * KT, KT), KT)

    def arrive(src):
        spot = pl.ds(pl.multiple_of(src * TOK, TOK), TOK)
        remote(kv8.at[0], kv_all.at[spot, :], kvs.at[0], kvr.at[src], x, y, 1 - c).wait_recv()

    def score(first, j, q2):
        chip, ds = keys_of(first, j)
        block = kv_all[ds, :]
        if first:
            vt_ref[0:64, ds] = block.T[64:128]
        return jnp.dot(block, q2, preferred_element_type=F32)

    def attend(kth):
        first = kth == 0
        tx = rem4(x + ORDER[kth])
        back = (4 - ORDER[kth]) % 4
        for i, (dx, dc) in enumerate(peers):
            if dx == back:
                x_copy(i).wait_recv()
        qs, accs, maxes = [], [], []
        for j in range(2):
            blk = x_all[2 * tx + j]
            qt = (blk[:, 0:128].astype(F32) * ATTN_SCALE).astype(BF16).T
            q2 = jnp.concatenate([qt[0:64], qt[64:128]], axis=1)
            q2 = jnp.concatenate([q2, jnp.zeros((64, 512), BF16)], axis=0)
            skv = blk[:, 128:256]
            s = jnp.dot(skv, q2, preferred_element_type=F32)
            srow = lax.broadcasted_iota(jnp.int32, (TOK, 512), 0)
            tcol = lax.broadcasted_iota(jnp.int32, (TOK, 512), 1) & 255
            visible = (srow <= tcol) & (srow < len_ref[2 * tx + j])
            s = jnp.where(visible, s * LOG2E, -jnp.inf)
            m = jnp.max(s, axis=0, keepdims=True)
            p = jnp.exp2(s - m)
            l = jnp.sum(p, axis=0, keepdims=True)
            acc = jnp.dot(skv.T[64:128], p.astype(BF16), preferred_element_type=F32)
            accs.append(jnp.concatenate([acc, jnp.broadcast_to(l, (16, 512))], axis=0))
            qs.append(q2)
            maxes.append(m)
        q2 = jnp.concatenate(qs, axis=1)
        acc = jnp.concatenate(accs, axis=1)
        m = jnp.concatenate(maxes, axis=1)
        n = PREFIX // KT
        if first:
            arrive(2 * (4 * x + y) + 1 - c)
        s_ref[0] = score(first, jnp.int32(0), q2)

        def step(i, carry):
            m, acc = carry
            for u in range(2):
                kk = 2 * i + u
                nxt = jnp.minimum(kk + 1, n - 1)
                if first:

                    @pl.when(kk + 1 < n)
                    def _():
                        chip, ds = keys_of(first, nxt)
                        arrive(2 * chip)
                        arrive(2 * chip + 1)

                s = s_ref[u]
                s_ref[1 - u] = score(first, nxt, q2)
                s = s * LOG2E
                mn = jnp.maximum(m, jnp.max(s, axis=0, keepdims=True))
                p = jnp.exp2(s - mn).astype(BF16)
                chip, ds = keys_of(first, kk)
                acc = acc * jnp.exp2(m - mn) + jnp.dot(vt_ref[:, ds], p, preferred_element_type=F32)
                m = mn
            return m, acc

        m, acc = lax.fori_loop(0, n // 2, step, (m, acc))
        out = acc[0:64] / acc[64:65]
        for j in range(2):
            ot = out[:, 512 * j : 512 * (j + 1)].T.astype(BF16)
            part_ref[2 * tx + j] = jnp.concatenate([ot[0:256], ot[256:512]], axis=1)

    def ctx_copy(i):
        tx, tc = peer(i)
        return remote(part_ref.at[2 * tx + tc], ctx_all.at[pos], cs.at[i], cr.at[i], tx, y, tc)

    for kth in range(4):
        if kth == 2:
            for slot_dy in (1, 3, 2):
                for cp in weight_copies(slot_dy, 1):
                    cp.wait_recv()
            for slot in range(3):
                for dz in (1, 3, 2):
                    for cp in column_copies(dz, slot):
                        cp.start()
        attend(kth)
        if kth == 0:
            ctx_all[pos] = part_ref[pos]
        for i, (dx, dc) in enumerate(peers):
            if dx == ORDER[kth]:
                ctx_copy(i).start()

    for i in range(7):
        ctx_copy(i).wait_recv()
    ctx = jnp.concatenate([ctx_all[h] for h in range(8)], axis=1)
    context_ref[...] = ctx
    projected = jnp.dot(ctx, wo_ref[...], preferred_element_type=F32)
    hidden = (tok_ref[...].astype(F32) + RESIDUAL_SCALE * projected).astype(BF16)
    hidden_ref[...] = hidden
    wide = hidden.astype(F32)
    mean_square = jnp.mean(wide * wide, axis=-1, keepdims=True)
    moe_buf[...] = (wide * lax.rsqrt(mean_square + NORM_EPS) * mgain_ref[...]).astype(BF16)

    def moe_copy(i, dx):
        return remote(moe_buf, moe_all.at[pos], ms.at[i], mr.at[i], rem4(x + dx), y, c)

    def relay_copy(i, spot, src):
        return remote(src, moe_all.at[spot], ms.at[3 + i], mr.at[3 + i], x, y, 1 - c)

    keep = pltpu.make_async_copy(moe_buf, moe_all.at[pos], own_sem.at[5])
    for i, dx in enumerate((1, 3, 2)):
        moe_copy(i, dx).start()
    relay_copy(3, pos, moe_buf).start()
    keep.start()
    relays = []
    for i, dx in enumerate((1, 3, 2)):
        moe_copy(i, dx).wait_recv()
        spot = 2 * rem4(x - dx) + c
        cp = relay_copy(i, spot, moe_all.at[spot])
        cp.start()
        relays.append(cp)

    keep.wait()
    for cp in own_copies():
        cp.wait()
    for i, dx in enumerate((1, 3, 2)):
        moe_copy(i, dx).wait_send()
    for cp in relays + [relay_copy(3, pos, moe_buf)]:
        cp.wait()
    for i in range(7):
        x_copy(i).wait_send()
        ctx_copy(i).wait_send()
        for cp in table_copies(i):
            cp.wait()
    kv_copy(0, 1 - c).wait_send()

    def kv_done(j, carry):
        for tc in (0, 1):
            kv_copy(j, tc).wait_send()
        return carry

    lax.fori_loop(1, 16, kv_done, 0)
    for dy in (1, 3, 2):
        for cp in weight_copies(dy, 1):
            cp.wait_send()
        for cp in weight_copies(dy, 0):
            cp.wait()
    for slot in range(3):
        for dz in (1, 3, 2):
            for cp in column_copies(dz, slot):
                cp.wait()


def front(*args):
    anywhere = pl.BlockSpec(memory_space=pl.ANY)
    dma = pltpu.SemaphoreType.DMA
    shape = jax.ShapeDtypeStruct
    return pl.pallas_call(
        front_kernel,
        out_shape=(
            shape((TOK, D), BF16), shape((TOK, D), BF16), shape((8, TOK, D), BF16),
            shape((8, 8, TOK), jnp.int32), shape((8, 8, TOK), F32),
            shape((4, D, FF), BF16), shape((4, D, FF), BF16), shape((4, FF, D), BF16),
        ),
        in_specs=vmem_specs(12) + [anywhere] * 5,
        out_specs=tuple(vmem_specs(2) + [anywhere] * 6),
        scratch_shapes=[
            pltpu.VMEM((8, TOK, 128), BF16),
            pltpu.VMEM((PREFIX, 128), BF16),
            pltpu.VMEM((8, TOK, 256), BF16),
            pltpu.VMEM((8, TOK, 256), BF16),
            pltpu.VMEM((80, PREFIX), BF16),
            pltpu.VMEM((2, KT, 1024), F32),
            pltpu.VMEM((8, TOK, 128), BF16),
            pltpu.VMEM((8, TOK, 128), BF16),
            pltpu.VMEM((TOK, D), BF16),
            dma((32,)), dma((32,)), dma((7,)), dma((7,)), dma((7,)), dma((7,)), dma((7,)), dma((7,)),
            dma((2, 7)), dma((2, 7)), dma((3, 3)), dma((3, 3)), dma((3, 3)), dma((3, 3)),
            dma((3, 3, 3)), dma((3, 3, 3)), dma((6,)),
        ],
        compiler_params=pltpu.CompilerParams(
            vmem_limit_bytes=VMEM_BYTES, collective_id=0, has_side_effects=True
        ),
        name="front",
    )(*args)


PHASES = (2, 1, 3, 0)


def tail_kernel(
    moe_all, ids_ref, rw_ref, g_all, u_all, d_all, mix_ref,
    x_v, g_v, u_v, d_v, rank_ref, wt_ref, rows_ref, eo_ref, pw_ref, keep_ref,
    pair_send, pair_recv, out_send, out_recv, xsem, wsem, ps, pr, os, orr,
):
    grp = lax.axis_index("grp")
    me = lax.axis_index("req")
    x, y, c = lax.div(me, 8), lax.rem(lax.div(me, 2), 4), lax.rem(me, 2)

    def remote(src, dst, send, recv, tx, tc):
        return pltpu.make_async_remote_copy(
            src_ref=src, dst_ref=dst, send_sem=send, recv_sem=recv,
            device_id=(grp, tx * 8 + y * 2 + tc), device_id_type=MESH_ID,
        )

    barrier = pltpu.get_barrier_semaphore()
    for tx, tc in [(x, 1 - c)] + [(rem4(x + dx), c) for dx in (1, 2, 3)]:
        pl.semaphore_signal(barrier, inc=1, device_id=(grp, tx * 8 + y * 2 + tc), device_id_type=MESH_ID)

    def two(k):
        return pl.ds(2 * rem4(x + PHASES[k]), 2)

    def load_rows(k):
        return pltpu.make_async_copy(moe_all.at[two(k)], x_v.at[k], xsem.at[k])

    def load_weights(e):
        return [
            pltpu.make_async_copy(src.at[e], dst.at[e], wsem.at[t, e])
            for t, (src, dst) in enumerate(((g_all, g_v), (u_all, u_v), (d_all, d_v)))
        ]

    load_rows(0).start()
    for e in range(4):
        for cp in load_weights(e):
            cp.start()
        if e < 3:
            load_rows(e + 1).start()

    tri = (
        lax.broadcasted_iota(jnp.int32, (TOK, TOK), 0) < lax.broadcasted_iota(jnp.int32, (TOK, TOK), 1)
    ).astype(BF16)
    for b in range(8):
        masks, weights = [], []
        for e in range(4):
            hits = ids_ref[b] == x * 8 + rem4(y + 1 + e) * 2 + c
            masks.append(jnp.max(hits.astype(F32), axis=0, keepdims=True))
            weights.append(jnp.sum(jnp.where(hits, rw_ref[b], 0.0), axis=0, keepdims=True))
        mask = jnp.concatenate(masks + [jnp.zeros((12, TOK), F32)], axis=0)
        rank = jnp.dot(mask.astype(BF16), tri, preferred_element_type=F32)
        rank_ref[b] = jnp.where(mask > 0, rank, -1.0)[0:8]
        wt_ref[b] = jnp.concatenate(weights + [jnp.zeros((4, TOK), F32)], axis=0)
    slot = lax.broadcasted_iota(jnp.int32, (CAP, TOK), 0).astype(F32)
    pl.semaphore_wait(barrier, 4)

    def pair_copy(k):
        return remote(pair_send.at[k], pair_recv.at[k], ps.at[k], pr.at[k], x, 1 - c)

    def out_copy(k):
        return remote(out_send.at[k], out_recv.at[k], os.at[k], orr.at[k], rem4(x + PHASES[k]), c)

    def finish(k):
        pair_copy(k).wait_recv()
        total = keep_ref[k % 2] + pair_recv[k].astype(F32)
        if k < 3:
            out_send[k] = total.astype(BF16)
            out_copy(k).start()
        return total

    for k in range(4):
        base = 2 * rem4(x + PHASES[k])
        load_rows(k).wait()

        def expert(e, carry):
            if k == 0:
                for cp in load_weights(e):
                    cp.wait()
            here = pl.ds(pl.multiple_of(e * CAP, CAP), CAP)
            for j in range(2):
                chosen = slot == rank_ref[base + j, pl.ds(e, 1), :]
                rows_ref[j * CAP : (j + 1) * CAP] = jnp.dot(
                    chosen.astype(BF16), x_v[k, j], preferred_element_type=F32
                ).astype(BF16)
                pw_ref[j, here] = jnp.where(chosen, wt_ref[base + j, pl.ds(e, 1), :], 0.0).astype(BF16)
            rows = rows_ref[...]
            gate = jnp.dot(rows, g_v[e], preferred_element_type=F32)
            up = jnp.dot(rows, u_v[e], preferred_element_type=F32)
            act = (jax.nn.silu(gate) * up).astype(BF16)
            out = jnp.dot(act, d_v[e], preferred_element_type=F32).astype(BF16)
            for j in range(2):
                eo_ref[j, here] = out[j * CAP : (j + 1) * CAP]
            if k > 0:

                @pl.when(e == 1)
                def _():
                    finish(k - 1)

            return carry

        lax.fori_loop(0, 4, expert, 0)

        def combine(j):
            return lax.dot_general(pw_ref[j], eo_ref[j], (((0,), (0,)), ((), ())), preferred_element_type=F32)

        pair_send[k] = combine(1 - c).astype(BF16)
        pair_copy(k).start()
        keep_ref[k % 2] = combine(c)
    total = finish(3)
    for k in range(3):
        out_copy(k).wait_recv()
        total = total + out_recv[k].astype(F32)
    mix_ref[...] = total.astype(BF16)
    for k in range(4):
        pair_copy(k).wait_send()
    for k in range(3):
        out_copy(k).wait_send()


def tail(moe_all, ids, rw, wg, wu, wd):
    anywhere = pl.BlockSpec(memory_space=pl.ANY)
    dma = pltpu.SemaphoreType.DMA
    return pl.pallas_call(
        tail_kernel,
        out_shape=jax.ShapeDtypeStruct((TOK, D), BF16),
        in_specs=[anywhere] + vmem_specs(2) + [anywhere] * 3,
        out_specs=vmem_specs(1)[0],
        scratch_shapes=[
            pltpu.VMEM((4, 2, TOK, D), BF16),
            pltpu.VMEM((4, D, FF), BF16),
            pltpu.VMEM((4, D, FF), BF16),
            pltpu.VMEM((4, FF, D), BF16),
            pltpu.VMEM((8, 8, TOK), F32),
            pltpu.VMEM((8, 8, TOK), F32),
            pltpu.VMEM((2 * CAP, D), BF16),
            pltpu.VMEM((2, 4 * CAP, D), BF16),
            pltpu.VMEM((2, 4 * CAP, TOK), BF16),
            pltpu.VMEM((2, TOK, D), F32),
            pltpu.VMEM((4, TOK, D), BF16),
            pltpu.VMEM((4, TOK, D), BF16),
            pltpu.VMEM((3, TOK, D), BF16),
            pltpu.VMEM((3, TOK, D), BF16),
            dma((4,)), dma((3, 4)), dma((4,)), dma((4,)), dma((3,)), dma((3,)),
        ],
        compiler_params=pltpu.CompilerParams(
            vmem_limit_bytes=VMEM_BYTES, collective_id=1, has_side_effects=True
        ),
        name="tail",
    )(moe_all, ids, rw, wg, wu, wd)


def local(
    tokens, attn_gain, w_query, w_key, w_value, w_out, prefix_keys, prefix_values,
    lengths, assignment, moe_gain, expert_ids, route_weights, w_gate, w_up, w_down,
):
    me = lax.axis_index("req")
    y_pos = (me // 2) % 4
    row = jnp.arange(8, dtype=jnp.int32)
    members = (row // 2) * 8 + y_pos * 2 + row % 2
    numbers = jnp.arange(32, dtype=jnp.int32)
    request = jnp.sum(jnp.where(members[:, None] == numbers[None, :], assignment[0][None, :], 0), axis=1)
    lens = jnp.sum(jnp.where(request[:, None] == numbers[None, :], lengths[0][None, :], 0), axis=1)
    lens = jnp.broadcast_to(lens[:, None, None], (8, 1, 512))
    cos, sin = rope_tables()
    context, hidden, moe_all, ids, rw, wg, wu, wd = front(
        tokens[0], attn_gain[None], w_query, w_key, w_value, w_out, moe_gain[None], cos, sin,
        prefix_keys[0], prefix_values[0], lens, expert_ids[0].T, route_weights[0].T, w_gate, w_up, w_down,
    )
    expert_mix = tail(moe_all, ids, rw, wg, wu, wd)
    return (context[None], hidden[None], expert_mix[None])


def solution(mesh):
    placed = (
        P("grp", "req", None), P(), P(), P(), P(), P(),
        P("grp", "req", None), P("grp", "req", None), P("grp", None), P("grp", None),
        P(), P("grp", "req", None), P("grp", "req", None),
        P("req", None, None), P("req", None, None), P("req", None, None),
    )
    return jax.shard_map(
        local,
        mesh=mesh,
        in_specs=placed,
        out_specs=(P("grp", "req", None), P("grp", "req", None), P("grp", "req", None)),
        check_vma=False,
    )
```

```python
import functools

import jax
import jax.numpy as jnp
import numpy as np
from jax import lax
from jax.experimental import pallas as pl
from jax.experimental.pallas import tpu as pltpu
from jax.sharding import PartitionSpec as P

HD = 64
CAP = 96
PREFIX = 8192
TOK = 256
D = 1024
FF = 512
NORM_EPS = 1e-06
ATTN_SCALE = 0.015625
RESIDUAL_SCALE = 0.22
ROPE_BASE = 10000.0
LOG2E = 1.4426950408889634
VMEM_BYTES = 60000 * 1024
BF16 = jnp.bfloat16
F32 = jnp.float32


def rope_tables():
    half = HD // 2
    freq = np.float32(ROPE_BASE) ** (-(np.arange(half, dtype=np.float32) * 2.0 / HD))
    pos = (PREFIX + np.arange(TOK)).astype(np.float32)
    angles = (pos[:, None] * freq.astype(np.float32)[None, :]).astype(np.float64)
    cos, sin = np.cos(angles), np.sin(angles)
    cos128 = np.concatenate([cos] * 4, axis=1).astype(np.float32)
    sin128 = np.concatenate([-sin, sin, -sin, sin], axis=1).astype(np.float32)
    return cos128, sin128


def vmem_specs(n):
    return [pl.BlockSpec(memory_space=pltpu.VMEM)] * n


def params():
    return pltpu.CompilerParams(vmem_limit_bytes=VMEM_BYTES)


MESH_ID = pl.DeviceIdType.MESH
KT = 512
ORDER = (0, 1, 3, 2)
HALF = 8
WIDE = ((384, 160), (384, 160), (192, 80))


def rem4(v):
    return lax.rem(v + 4, 4)


def front_kernel(
    tok_ref, again_ref, wq_ref, wk_ref, wv_ref, wo_ref, mgain_ref, cos_ref, sin_ref, pk_ref, pv_ref, len_ref,
    ids_in, rw_in, g_in, u_in, d_in,
    context_ref, hidden_ref, moe_all, ids_all, rw_all, g_all, u_all, d_all,
    kv8, kv_all, x_send, x_all, vt_ref, s_ref, q_st, m_st, acc_st, part_ref, ctx_all, moe_buf,
    kvs, kvr, xs, xr, cs, cr, ms, mr, ts, tr, ws, wr, vs, vr, zs, zr, own_sem,
):
    grp = lax.axis_index("grp")
    me = lax.axis_index("req")
    x, y, c = lax.div(me, 8), lax.rem(lax.div(me, 2), 4), lax.rem(me, 2)
    pos = 2 * x + c

    def remote(src, dst, send, recv, tx, ty, tc, tg=None):
        where = (grp if tg is None else tg, tx * 8 + ty * 2 + tc)
        return pltpu.make_async_remote_copy(
            src_ref=src, dst_ref=dst, send_sem=send, recv_sem=recv, device_id=where, device_id_type=MESH_ID
        )

    barrier = pltpu.get_barrier_semaphore()

    def greet(i, carry):
        pl.semaphore_signal(barrier, inc=1, device_id=(grp, lax.rem(me + i, 32)), device_id_type=MESH_ID)
        return carry

    lax.fori_loop(1, 32, greet, 0)
    for dz in (1, 2, 3):
        pl.semaphore_signal(barrier, inc=1, device_id=(rem4(grp + dz), me), device_id_type=MESH_ID)

    def own_copies():
        pairs = [(ids_in, ids_all.at[pos]), (rw_in, rw_all.at[pos])]
        return [pltpu.make_async_copy(a, b, own_sem.at[i]) for i, (a, b) in enumerate(pairs)]

    for cp in own_copies():
        cp.start()

    for pair in range(4):
        kr = pk_ref[:, 128 * pair : 128 * pair + 128]
        vr_ = pv_ref[:, 128 * pair : 128 * pair + 128]
        kv8[2 * pair] = jnp.concatenate([kr[:, 0:64], vr_[:, 0:64]], axis=1)
        kv8[2 * pair + 1] = jnp.concatenate([kr[:, 64:128], vr_[:, 64:128]], axis=1)
    mine = pl.ds(pl.multiple_of(me * TOK, TOK), TOK)
    kv_all[mine, :] = kv8[pos]
    pl.semaphore_wait(barrier, 34)

    def offset(half, j):
        t, u = lax.div(j, 4) - 2 * half, lax.rem(j, 4)
        side = 1 + 2 * lax.div(u, 2)
        if half == 0:
            dx = t * side
            return dx, (1 - t) * u + t * lax.rem(u, 2) * dx
        return (1 - t) * side + 2 * t, (1 - t) * (2 + lax.rem(u, 2) * (2 - side)) + t * u

    def kv_copy(half, j, tc):
        dx, dy = offset(half, j)
        tx, ty = lax.rem(x + dx, 4), lax.rem(y + dy, 4)
        return remote(kv8.at[2 * tx + tc], kv_all.at[mine, :], kvs.at[2 * j + tc], kvr.at[me], tx, ty, tc)

    def kv_each(half, what):
        def both(j, carry):
            for tc in (0, 1):
                what(kv_copy(half, j, tc))
            return carry

        if half == 0:
            what(remote(kv8.at[2 * x + 1 - c], kv_all.at[mine, :], kvs.at[0], kvr.at[me], x, y, 1 - c))
        lax.fori_loop(1 if half == 0 else HALF, HALF if half == 0 else 2 * HALF, both, 0)

    kv_each(0, lambda cp: cp.start())

    peers = [(0, 1)] + [(dx, dc) for dx in (1, 3, 2) for dc in (0, 1)]

    def peer(i):
        dx, dc = peers[i]
        return rem4(x + dx), lax.rem(c + dc, 2)

    def table_copies(i):
        tx, tc = peer(i)
        return (
            remote(ids_in, ids_all.at[pos], ts.at[0, i], tr.at[0, i], tx, y, tc),
            remote(rw_in, rw_all.at[pos], ts.at[1, i], tr.at[1, i], tx, y, tc),
        )

    for i in range(7):
        for cp in table_copies(i):
            cp.start()

    stacks = ((g_in, g_all), (u_in, u_all), (d_in, d_all))

    def quarter_rows(t):
        straight, quarter = WIDE[t]
        return pl.ds(pl.multiple_of(straight + grp * quarter, 16), quarter)

    def weight_copies(dy, part):
        out = []
        for t, (src, dst) in enumerate(stacks):
            rows = quarter_rows(t) if part else pl.ds(0, WIDE[t][0])
            sems = (vs, vr) if part else (ws, wr)
            out.append(
                remote(src.at[0, rows, :], dst.at[3 - dy, rows, :], sems[0].at[dy - 1, t], sems[1].at[dy - 1, t],
                       x, rem4(y + dy), c)
            )
        return out

    def column_copies(dz, slot):
        out = []
        for t, (src, dst) in enumerate(stacks):
            rows = quarter_rows(t)
            out.append(
                remote(dst.at[slot, rows, :], dst.at[slot, rows, :], zs.at[dz - 1, slot, t], zr.at[dz - 1, slot, t],
                       x, y, c, rem4(grp + dz))
            )
        return out

    for dy in (1, 3, 2):
        for cp in weight_copies(dy, 1):
            cp.start()

    rows = tok_ref[...].astype(F32)
    mean_square = jnp.mean(rows * rows, axis=-1, keepdims=True)
    normed = (rows * lax.rsqrt(mean_square + NORM_EPS) * again_ref[...]).astype(BF16)
    cos, sin = cos_ref[...], sin_ref[...]
    low = (lax.broadcasted_iota(jnp.int32, (TOK, 128), 1) & 32) == 0

    def rotate(part):
        other = jnp.where(low, pltpu.roll(part, 96, 1), pltpu.roll(part, 32, 1))
        return (part * cos + other * sin).astype(BF16)

    q = jnp.dot(normed, wq_ref[...], preferred_element_type=F32)
    k = jnp.dot(normed, wk_ref[...], preferred_element_type=F32)
    v = jnp.dot(normed, wv_ref[...], preferred_element_type=F32).astype(BF16)
    for h in range(8):
        x_send[h, :, 0:128] = rotate(q[:, 128 * h : 128 * h + 128])
    for pair in range(4):
        kr = rotate(k[:, 128 * pair : 128 * pair + 128])
        vr_ = v[:, 128 * pair : 128 * pair + 128]
        x_send[2 * pair, :, 128:256] = jnp.concatenate([kr[:, 0:64], vr_[:, 0:64]], axis=1)
        x_send[2 * pair + 1, :, 128:256] = jnp.concatenate([kr[:, 64:128], vr_[:, 64:128]], axis=1)
    x_all[pos] = x_send[pos]

    def x_copy(i):
        tx, tc = peer(i)
        return remote(x_send.at[2 * tx + tc], x_all.at[pos], xs.at[i], xr.at[i], tx, y, tc)

    for i in range(7):
        x_copy(i).start()
    kv_each(1, lambda cp: cp.start())
    for dy in (1, 3, 2):
        for cp in weight_copies(dy, 0):
            cp.start()

    vt_ref[64:80, :] = jnp.ones((16, PREFIX), BF16)

    def keys_of(half, j):
        dx, dy = offset(half, j)
        chip = lax.rem(x + 4 - dx, 4) * 4 + lax.rem(y + 4 - dy, 4)
        return chip, pl.ds(pl.multiple_of(chip * KT, KT), KT)

    def arrive(src):
        spot = pl.ds(pl.multiple_of(src * TOK, TOK), TOK)
        remote(kv8.at[0], kv_all.at[spot, :], kvs.at[0], kvr.at[src], x, y, 1 - c).wait_recv()

    def score(fresh, half, j, q2):
        chip, ds = keys_of(half, j)
        block = kv_all[ds, :]
        if fresh:
            vt_ref[0:64, ds] = block.T[64:128]
        return jnp.dot(block, q2, preferred_element_type=F32)

    def begin(kth):
        tx = rem4(x + ORDER[kth])
        back = (4 - ORDER[kth]) % 4
        for i, (dx, dc) in enumerate(peers):
            if dx == back:
                x_copy(i).wait_recv()
        for j in range(2):
            blk = x_all[2 * tx + j]
            qt = (blk[:, 0:128].astype(F32) * ATTN_SCALE).astype(BF16).T
            q2 = jnp.concatenate([qt[0:64], qt[64:128]], axis=1)
            q2 = jnp.concatenate([q2, jnp.zeros((64, 512), BF16)], axis=0)
            skv = blk[:, 128:256]
            s = jnp.dot(skv, q2, preferred_element_type=F32)
            srow = lax.broadcasted_iota(jnp.int32, (TOK, 512), 0)
            tcol = lax.broadcasted_iota(jnp.int32, (TOK, 512), 1) & 255
            visible = (srow <= tcol) & (srow < len_ref[2 * tx + j])
            s = jnp.where(visible, s * LOG2E, -jnp.inf)
            m = jnp.max(s, axis=0, keepdims=True)
            p = jnp.exp2(s - m)
            l = jnp.sum(p, axis=0, keepdims=True)
            acc = jnp.dot(skv.T[64:128], p.astype(BF16), preferred_element_type=F32)
            cols = slice(512 * j, 512 * (j + 1))
            q_st[kth, :, cols] = q2
            m_st[kth, :, cols] = m
            acc_st[kth, 0:64, cols] = acc
            acc_st[kth, 64:80, cols] = jnp.broadcast_to(l, (16, 512))

    def attend(kth, half, fresh):
        q2 = q_st[kth]
        lo, hi = half * HALF, half * HALF + HALF
        if fresh and half == 0:
            arrive(2 * (4 * x + y) + 1 - c)
        elif fresh:
            chip, ds = keys_of(half, jnp.int32(lo))
            arrive(2 * chip)
            arrive(2 * chip + 1)
        s_ref[0] = score(fresh, half, jnp.int32(lo), q2)

        def step(i, carry):
            m, acc = carry
            for u in range(2):
                kk = lo + 2 * i + u
                nxt = jnp.minimum(kk + 1, hi - 1)
                if fresh:

                    @pl.when(kk + 1 < hi)
                    def _():
                        chip, ds = keys_of(half, nxt)
                        arrive(2 * chip)
                        arrive(2 * chip + 1)

                s = s_ref[u]
                s_ref[1 - u] = score(fresh, half, nxt, q2)
                s = s * LOG2E
                mn = jnp.maximum(m, jnp.max(s, axis=0, keepdims=True))
                p = jnp.exp2(s - mn).astype(BF16)
                chip, ds = keys_of(half, kk)
                acc = acc * jnp.exp2(m - mn) + jnp.dot(vt_ref[:, ds], p, preferred_element_type=F32)
                m = mn
            return m, acc

        m, acc = lax.fori_loop(0, HALF // 2, step, (m_st[kth], acc_st[kth]))
        if half == 0:
            m_st[kth] = m
            acc_st[kth] = acc
            return
        tx = rem4(x + ORDER[kth])
        out = acc[0:64] / acc[64:65]
        for j in range(2):
            ot = out[:, 512 * j : 512 * (j + 1)].T.astype(BF16)
            part_ref[2 * tx + j] = jnp.concatenate([ot[0:256], ot[256:512]], axis=1)

    def ctx_copy(i):
        tx, tc = peer(i)
        return remote(part_ref.at[2 * tx + tc], ctx_all.at[pos], cs.at[i], cr.at[i], tx, y, tc)

    for kth in range(4):
        if kth == 3:
            for slot_dy in (1, 3, 2):
                for cp in weight_copies(slot_dy, 1):
                    cp.wait_recv()
            for slot in range(3):
                for dz in (1, 3, 2):
                    for cp in column_copies(dz, slot):
                        cp.start()
        begin(kth)
        attend(kth, 0, kth == 0)
    for kth in (3, 1, 2, 0):
        attend(kth, 1, kth == 3)
        if kth == 0:
            ctx_all[pos] = part_ref[pos]
        for i, (dx, dc) in enumerate(peers):
            if dx == ORDER[kth]:
                ctx_copy(i).start()

    for i in range(7):
        ctx_copy(i).wait_recv()
    ctx = jnp.concatenate([ctx_all[h] for h in range(8)], axis=1)
    context_ref[...] = ctx
    projected = jnp.dot(ctx, wo_ref[...], preferred_element_type=F32)
    hidden = (tok_ref[...].astype(F32) + RESIDUAL_SCALE * projected).astype(BF16)
    hidden_ref[...] = hidden
    wide = hidden.astype(F32)
    mean_square = jnp.mean(wide * wide, axis=-1, keepdims=True)
    moe_buf[...] = (wide * lax.rsqrt(mean_square + NORM_EPS) * mgain_ref[...]).astype(BF16)

    def moe_copy(i, dx):
        return remote(moe_buf, moe_all.at[pos], ms.at[i], mr.at[i], rem4(x + dx), y, c)

    def relay_copy(i, spot, src):
        return remote(src, moe_all.at[spot], ms.at[3 + i], mr.at[3 + i], x, y, 1 - c)

    keep = pltpu.make_async_copy(moe_buf, moe_all.at[pos], own_sem.at[2])
    for i, dx in enumerate((1, 3, 2)):
        moe_copy(i, dx).start()
    relay_copy(3, pos, moe_buf).start()
    keep.start()
    relays = []
    for i, dx in enumerate((1, 3, 2)):
        moe_copy(i, dx).wait_recv()
        spot = 2 * rem4(x - dx) + c
        cp = relay_copy(i, spot, moe_all.at[spot])
        cp.start()
        relays.append(cp)

    keep.wait()
    for cp in own_copies():
        cp.wait()
    for i, dx in enumerate((1, 3, 2)):
        moe_copy(i, dx).wait_send()
    for cp in relays + [relay_copy(3, pos, moe_buf)]:
        cp.wait()
    for i in range(7):
        x_copy(i).wait_send()
        ctx_copy(i).wait_send()
        for cp in table_copies(i):
            cp.wait()
    for half in (0, 1):
        kv_each(half, lambda cp: cp.wait_send())
    for dy in (1, 3, 2):
        for cp in weight_copies(dy, 1):
            cp.wait_send()
        for cp in weight_copies(dy, 0):
            cp.wait()
    for slot in range(3):
        for dz in (1, 3, 2):
            for cp in column_copies(dz, slot):
                cp.wait()


def front(*args):
    anywhere = pl.BlockSpec(memory_space=pl.ANY)
    dma = pltpu.SemaphoreType.DMA
    shape = jax.ShapeDtypeStruct
    return pl.pallas_call(
        front_kernel,
        out_shape=(
            shape((TOK, D), BF16), shape((TOK, D), BF16), shape((8, TOK, D), BF16),
            shape((8, 8, TOK), jnp.int32), shape((8, 8, TOK), F32),
            shape((3, D, FF), BF16), shape((3, D, FF), BF16), shape((3, FF, D), BF16),
        ),
        in_specs=vmem_specs(12) + [anywhere] * 5,
        out_specs=tuple(vmem_specs(2) + [anywhere] * 6),
        scratch_shapes=[
            pltpu.VMEM((8, TOK, 128), BF16),
            pltpu.VMEM((PREFIX, 128), BF16),
            pltpu.VMEM((8, TOK, 256), BF16),
            pltpu.VMEM((8, TOK, 256), BF16),
            pltpu.VMEM((80, PREFIX), BF16),
            pltpu.VMEM((2, KT, 1024), F32),
            pltpu.VMEM((4, 128, 1024), BF16),
            pltpu.VMEM((4, 1, 1024), F32),
            pltpu.VMEM((4, 80, 1024), F32),
            pltpu.VMEM((8, TOK, 128), BF16),
            pltpu.VMEM((8, TOK, 128), BF16),
            pltpu.VMEM((TOK, D), BF16),
            dma((32,)), dma((32,)), dma((7,)), dma((7,)), dma((7,)), dma((7,)), dma((7,)), dma((7,)),
            dma((2, 7)), dma((2, 7)), dma((3, 3)), dma((3, 3)), dma((3, 3)), dma((3, 3)),
            dma((3, 3, 3)), dma((3, 3, 3)), dma((3,)),
        ],
        compiler_params=pltpu.CompilerParams(
            vmem_limit_bytes=VMEM_BYTES, collective_id=0, has_side_effects=True
        ),
        name="front",
    )(*args)


PHASES = (2, 1, 3, 0)


def tail_kernel(
    moe_all, ids_ref, rw_ref, g_in, u_in, d_in, g_all, u_all, d_all, mix_ref,
    x_v, g_v, u_v, d_v, rank_ref, wt_ref, rows_ref, eo_ref, pw_ref, keep_ref,
    pair_send, pair_recv, out_send, out_recv, xsem, wsem, ps, pr, os, orr,
):
    grp = lax.axis_index("grp")
    me = lax.axis_index("req")
    x, y, c = lax.div(me, 8), lax.rem(lax.div(me, 2), 4), lax.rem(me, 2)

    def remote(src, dst, send, recv, tx, tc):
        return pltpu.make_async_remote_copy(
            src_ref=src, dst_ref=dst, send_sem=send, recv_sem=recv,
            device_id=(grp, tx * 8 + y * 2 + tc), device_id_type=MESH_ID,
        )

    barrier = pltpu.get_barrier_semaphore()
    for tx, tc in [(x, 1 - c)] + [(rem4(x + dx), c) for dx in (1, 2, 3)]:
        pl.semaphore_signal(barrier, inc=1, device_id=(grp, tx * 8 + y * 2 + tc), device_id_type=MESH_ID)

    def two(k):
        return pl.ds(2 * rem4(x + PHASES[k]), 2)

    def load_rows(k):
        return pltpu.make_async_copy(moe_all.at[two(k)], x_v.at[k], xsem.at[k])

    def load_weights(e, own=False):
        sources = (g_in, u_in, d_in) if own else (g_all, u_all, d_all)
        return [
            pltpu.make_async_copy(src.at[0 if own else e], dst.at[e], wsem.at[t, e])
            for t, (src, dst) in enumerate(zip(sources, (g_v, u_v, d_v)))
        ]

    load_rows(0).start()
    for e in range(4):
        for cp in load_weights(e, e == 3):
            cp.start()
        if e < 3:
            load_rows(e + 1).start()

    tri = (
        lax.broadcasted_iota(jnp.int32, (TOK, TOK), 0) < lax.broadcasted_iota(jnp.int32, (TOK, TOK), 1)
    ).astype(BF16)
    for b in range(8):
        masks, weights = [], []
        for e in range(4):
            hits = ids_ref[b] == x * 8 + rem4(y + 1 + e) * 2 + c
            masks.append(jnp.max(hits.astype(F32), axis=0, keepdims=True))
            weights.append(jnp.sum(jnp.where(hits, rw_ref[b], 0.0), axis=0, keepdims=True))
        mask = jnp.concatenate(masks + [jnp.zeros((12, TOK), F32)], axis=0)
        rank = jnp.dot(mask.astype(BF16), tri, preferred_element_type=F32)
        rank_ref[b] = jnp.where(mask > 0, rank, -1.0)[0:8]
        wt_ref[b] = jnp.concatenate(weights + [jnp.zeros((4, TOK), F32)], axis=0)
    slot = lax.broadcasted_iota(jnp.int32, (CAP, TOK), 0).astype(F32)
    pl.semaphore_wait(barrier, 4)

    def pair_copy(k):
        return remote(pair_send.at[k], pair_recv.at[k], ps.at[k], pr.at[k], x, 1 - c)

    def out_copy(k):
        return remote(out_send.at[k], out_recv.at[k], os.at[k], orr.at[k], rem4(x + PHASES[k]), c)

    def finish(k):
        pair_copy(k).wait_recv()
        total = keep_ref[k % 2] + pair_recv[k].astype(F32)
        if k < 3:
            out_send[k] = total.astype(BF16)
            out_copy(k).start()
        return total

    for k in range(4):
        base = 2 * rem4(x + PHASES[k])
        load_rows(k).wait()

        def expert(e, carry):
            if k == 0:
                for src, dst, t in ((g_in, g_v, 0), (u_in, u_v, 1), (d_in, d_v, 2)):
                    pltpu.make_async_copy(src.at[0], dst.at[e], wsem.at[t, e]).wait()
            here = pl.ds(pl.multiple_of(e * CAP, CAP), CAP)
            for j in range(2):
                chosen = slot == rank_ref[base + j, pl.ds(e, 1), :]
                rows_ref[j * CAP : (j + 1) * CAP] = jnp.dot(
                    chosen.astype(BF16), x_v[k, j], preferred_element_type=F32
                ).astype(BF16)
                pw_ref[j, here] = jnp.where(chosen, wt_ref[base + j, pl.ds(e, 1), :], 0.0).astype(BF16)
            rows = rows_ref[...]
            gate = jnp.dot(rows, g_v[e], preferred_element_type=F32)
            up = jnp.dot(rows, u_v[e], preferred_element_type=F32)
            act = (jax.nn.silu(gate) * up).astype(BF16)
            out = jnp.dot(act, d_v[e], preferred_element_type=F32).astype(BF16)
            for j in range(2):
                eo_ref[j, here] = out[j * CAP : (j + 1) * CAP]
            if k > 0:

                @pl.when(e == 1)
                def _():
                    finish(k - 1)

            return carry

        lax.fori_loop(0, 4, expert, 0)

        def combine(j):
            return lax.dot_general(pw_ref[j], eo_ref[j], (((0,), (0,)), ((), ())), preferred_element_type=F32)

        pair_send[k] = combine(1 - c).astype(BF16)
        pair_copy(k).start()
        keep_ref[k % 2] = combine(c)
    total = finish(3)
    for k in range(3):
        out_copy(k).wait_recv()
        total = total + out_recv[k].astype(F32)
    mix_ref[...] = total.astype(BF16)
    for k in range(4):
        pair_copy(k).wait_send()
    for k in range(3):
        out_copy(k).wait_send()


def tail(moe_all, ids, rw, own, gathered):
    anywhere = pl.BlockSpec(memory_space=pl.ANY)
    dma = pltpu.SemaphoreType.DMA
    return pl.pallas_call(
        tail_kernel,
        out_shape=jax.ShapeDtypeStruct((TOK, D), BF16),
        in_specs=[anywhere] + vmem_specs(2) + [anywhere] * 6,
        out_specs=vmem_specs(1)[0],
        scratch_shapes=[
            pltpu.VMEM((4, 2, TOK, D), BF16),
            pltpu.VMEM((4, D, FF), BF16),
            pltpu.VMEM((4, D, FF), BF16),
            pltpu.VMEM((4, FF, D), BF16),
            pltpu.VMEM((8, 8, TOK), F32),
            pltpu.VMEM((8, 8, TOK), F32),
            pltpu.VMEM((2 * CAP, D), BF16),
            pltpu.VMEM((2, 4 * CAP, D), BF16),
            pltpu.VMEM((2, 4 * CAP, TOK), BF16),
            pltpu.VMEM((2, TOK, D), F32),
            pltpu.VMEM((4, TOK, D), BF16),
            pltpu.VMEM((4, TOK, D), BF16),
            pltpu.VMEM((3, TOK, D), BF16),
            pltpu.VMEM((3, TOK, D), BF16),
            dma((4,)), dma((3, 4)), dma((4,)), dma((4,)), dma((3,)), dma((3,)),
        ],
        compiler_params=pltpu.CompilerParams(
            vmem_limit_bytes=VMEM_BYTES, collective_id=1, has_side_effects=True
        ),
        name="tail",
    )(moe_all, ids, rw, *own, *gathered)


def local(
    tokens, attn_gain, w_query, w_key, w_value, w_out, prefix_keys, prefix_values,
    lengths, assignment, moe_gain, expert_ids, route_weights, w_gate, w_up, w_down,
):
    me = lax.axis_index("req")
    y_pos = (me // 2) % 4
    row = jnp.arange(8, dtype=jnp.int32)
    members = (row // 2) * 8 + y_pos * 2 + row % 2
    numbers = jnp.arange(32, dtype=jnp.int32)
    request = jnp.sum(jnp.where(members[:, None] == numbers[None, :], assignment[0][None, :], 0), axis=1)
    lens = jnp.sum(jnp.where(request[:, None] == numbers[None, :], lengths[0][None, :], 0), axis=1)
    lens = jnp.broadcast_to(lens[:, None, None], (8, 1, 512))
    cos, sin = rope_tables()
    context, hidden, moe_all, ids, rw, wg, wu, wd = front(
        tokens[0], attn_gain[None], w_query, w_key, w_value, w_out, moe_gain[None], cos, sin,
        prefix_keys[0], prefix_values[0], lens, expert_ids[0].T, route_weights[0].T, w_gate, w_up, w_down,
    )
    expert_mix = tail(moe_all, ids, rw, (w_gate, w_up, w_down), (wg, wu, wd))
    return (context[None], hidden[None], expert_mix[None])


def solution(mesh):
    placed = (
        P("grp", "req", None), P(), P(), P(), P(), P(),
        P("grp", "req", None), P("grp", "req", None), P("grp", None), P("grp", None),
        P(), P("grp", "req", None), P("grp", "req", None),
        P("req", None, None), P("req", None, None), P("req", None, None),
    )
    return jax.shard_map(
        local,
        mesh=mesh,
        in_specs=placed,
        out_specs=(P("grp", "req", None), P("grp", "req", None), P("grp", "req", None)),
        check_vma=False,
    )
```

```python
import functools

import jax
import jax.numpy as jnp
import numpy as np
from jax import lax
from jax.experimental import pallas as pl
from jax.experimental.pallas import tpu as pltpu
from jax.sharding import PartitionSpec as P

HD = 64
CAP = 96
PREFIX = 8192
TOK = 256
D = 1024
FF = 512
NORM_EPS = 1e-06
ATTN_SCALE = 0.015625
RESIDUAL_SCALE = 0.22
ROPE_BASE = 10000.0
LOG2E = 1.4426950408889634
VMEM_BYTES = 60000 * 1024
BF16 = jnp.bfloat16
F32 = jnp.float32


def rope_tables():
    half = HD // 2
    freq = np.float32(ROPE_BASE) ** (-(np.arange(half, dtype=np.float32) * 2.0 / HD))
    pos = (PREFIX + np.arange(TOK)).astype(np.float32)
    angles = (pos[:, None] * freq.astype(np.float32)[None, :]).astype(np.float64)
    cos, sin = np.cos(angles), np.sin(angles)
    cos128 = np.concatenate([cos] * 4, axis=1).astype(np.float32)
    sin128 = np.concatenate([-sin, sin, -sin, sin], axis=1).astype(np.float32)
    return cos128, sin128


def vmem_specs(n):
    return [pl.BlockSpec(memory_space=pltpu.VMEM)] * n


def params():
    return pltpu.CompilerParams(vmem_limit_bytes=VMEM_BYTES)


MESH_ID = pl.DeviceIdType.MESH
KT = 512
ORDER = (0, 1, 3, 2)
HALF = 8
WIDE = ((384, 160), (384, 160), (192, 80))


def rem4(v):
    return lax.rem(v + 4, 4)


def front_kernel(
    tok_ref, again_ref, wq_ref, wk_ref, wv_ref, wo_ref, mgain_ref, cos_ref, sin_ref, pk_ref, pv_ref, assign_ref, lengths_ref,
    ids_in, rw_in, g_in, u_in, d_in,
    context_ref, hidden_ref, moe_all, ids_all, rw_all, g_all, u_all, d_all,
    kv8, kv_all, x_send, x_all, vt_ref, s_ref, q_st, m_st, acc_st, part_ref, ctx_all, moe_buf,
    kvs, kvr, xs, xr, cs, cr, ms, mr, ts, tr, ws, wr, vs, vr, zs, zr, own_sem,
):
    grp = lax.axis_index("grp")
    me = lax.axis_index("req")
    x, y, c = lax.div(me, 8), lax.rem(lax.div(me, 2), 4), lax.rem(me, 2)
    pos = 2 * x + c

    def remote(src, dst, send, recv, tx, ty, tc, tg=None):
        where = (grp if tg is None else tg, tx * 8 + ty * 2 + tc)
        return pltpu.make_async_remote_copy(
            src_ref=src, dst_ref=dst, send_sem=send, recv_sem=recv, device_id=where, device_id_type=MESH_ID
        )

    barrier = pltpu.get_barrier_semaphore()

    def greet(i, carry):
        pl.semaphore_signal(barrier, inc=1, device_id=(grp, lax.rem(me + i, 32)), device_id_type=MESH_ID)
        return carry

    lax.fori_loop(1, 32, greet, 0)
    for dz in (1, 2, 3):
        pl.semaphore_signal(barrier, inc=1, device_id=(rem4(grp + dz), me), device_id_type=MESH_ID)

    def own_copies():
        pairs = [(ids_in, ids_all.at[pos]), (rw_in, rw_all.at[pos])]
        return [pltpu.make_async_copy(a, b, own_sem.at[i]) for i, (a, b) in enumerate(pairs)]

    for cp in own_copies():
        cp.start()

    for pair in range(4):
        kr = pk_ref[:, 128 * pair : 128 * pair + 128]
        vr_ = pv_ref[:, 128 * pair : 128 * pair + 128]
        kv8[2 * pair] = jnp.concatenate([kr[:, 0:64], vr_[:, 0:64]], axis=1)
        kv8[2 * pair + 1] = jnp.concatenate([kr[:, 64:128], vr_[:, 64:128]], axis=1)
    mine = pl.ds(pl.multiple_of(me * TOK, TOK), TOK)
    kv_all[mine, :] = kv8[pos]
    pl.semaphore_wait(barrier, 34)

    def offset(half, j):
        t, u = lax.div(j, 4) - 2 * half, lax.rem(j, 4)
        side = 1 + 2 * lax.div(u, 2)
        if half == 0:
            dx = t * side
            return dx, (1 - t) * u + t * lax.rem(u, 2) * dx
        return (1 - t) * side + 2 * t, (1 - t) * (2 + lax.rem(u, 2) * (2 - side)) + t * u

    def kv_copy(half, j, tc):
        dx, dy = offset(half, j)
        tx, ty = lax.rem(x + dx, 4), lax.rem(y + dy, 4)
        return remote(kv8.at[2 * tx + tc], kv_all.at[mine, :], kvs.at[2 * j + tc], kvr.at[me], tx, ty, tc)

    def kv_each(half, what):
        def both(j, carry):
            for tc in (0, 1):
                what(kv_copy(half, j, tc))
            return carry

        if half == 0:
            what(remote(kv8.at[2 * x + 1 - c], kv_all.at[mine, :], kvs.at[0], kvr.at[me], x, y, 1 - c))
        lax.fori_loop(1 if half == 0 else HALF, HALF if half == 0 else 2 * HALF, both, 0)

    kv_each(0, lambda cp: cp.start())

    peers = [(0, 1)] + [(dx, dc) for dx in (1, 3, 2) for dc in (0, 1)]

    def peer(i):
        dx, dc = peers[i]
        return rem4(x + dx), lax.rem(c + dc, 2)

    def table_copies(i):
        tx, tc = peer(i)
        return (
            remote(ids_in, ids_all.at[pos], ts.at[0, i], tr.at[0, i], tx, y, tc),
            remote(rw_in, rw_all.at[pos], ts.at[1, i], tr.at[1, i], tx, y, tc),
        )

    for i in range(7):
        for cp in table_copies(i):
            cp.start()

    stacks = ((g_in, g_all), (u_in, u_all), (d_in, d_all))

    def quarter_rows(t):
        straight, quarter = WIDE[t]
        return pl.ds(pl.multiple_of(straight + grp * quarter, 16), quarter)

    def weight_copies(dy, part, only=(0, 1, 2)):
        out = []
        for t in only:
            src, dst = stacks[t]
            rows = quarter_rows(t) if part else pl.ds(0, WIDE[t][0])
            sems = (vs, vr) if part else (ws, wr)
            out.append(
                remote(src.at[0, rows, :], dst.at[3 - dy, rows, :], sems[0].at[dy - 1, t], sems[1].at[dy - 1, t],
                       x, rem4(y + dy), c)
            )
        return out

    def column_copies(dz, slot, only=(0, 1, 2)):
        out = []
        for t in only:
            src, dst = stacks[t]
            rows = quarter_rows(t)
            out.append(
                remote(dst.at[slot, rows, :], dst.at[slot, rows, :], zs.at[dz - 1, slot, t], zr.at[dz - 1, slot, t],
                       x, y, c, rem4(grp + dz))
            )
        return out

    def weights_start(part, only):
        for dy in (1, 3, 2):
            for cp in weight_copies(dy, part, only):
                cp.start()

    def column_start(only):
        for dy in (1, 3, 2):
            for cp in weight_copies(dy, 1, only):
                cp.wait_recv()
        for slot in range(3):
            for dz in (1, 3, 2):
                for cp in column_copies(dz, slot, only):
                    cp.start()

    weights_start(1, (0,))

    rows = tok_ref[...].astype(F32)
    mean_square = jnp.mean(rows * rows, axis=-1, keepdims=True)
    normed = (rows * lax.rsqrt(mean_square + NORM_EPS) * again_ref[...]).astype(BF16)
    cos, sin = cos_ref[...], sin_ref[...]
    low = (lax.broadcasted_iota(jnp.int32, (TOK, 128), 1) & 32) == 0

    def rotate(part):
        other = jnp.where(low, pltpu.roll(part, 96, 1), pltpu.roll(part, 32, 1))
        return (part * cos + other * sin).astype(BF16)

    q = jnp.dot(normed, wq_ref[...], preferred_element_type=F32)
    k = jnp.dot(normed, wk_ref[...], preferred_element_type=F32)
    v = jnp.dot(normed, wv_ref[...], preferred_element_type=F32).astype(BF16)
    for h in range(8):
        x_send[h, :, 0:128] = rotate(q[:, 128 * h : 128 * h + 128])
    for pair in range(4):
        kr = rotate(k[:, 128 * pair : 128 * pair + 128])
        vr_ = v[:, 128 * pair : 128 * pair + 128]
        x_send[2 * pair, :, 128:256] = jnp.concatenate([kr[:, 0:64], vr_[:, 0:64]], axis=1)
        x_send[2 * pair + 1, :, 128:256] = jnp.concatenate([kr[:, 64:128], vr_[:, 64:128]], axis=1)
    x_all[pos] = x_send[pos]

    def x_copy(i):
        tx, tc = peer(i)
        return remote(x_send.at[2 * tx + tc], x_all.at[pos], xs.at[i], xr.at[i], tx, y, tc)

    for i in range(7):
        x_copy(i).start()
    kv_each(1, lambda cp: cp.start())
    vt_ref[64:80, :] = jnp.ones((16, PREFIX), BF16)

    def keys_of(half, j):
        dx, dy = offset(half, j)
        chip = lax.rem(x + 4 - dx, 4) * 4 + lax.rem(y + 4 - dy, 4)
        return chip, pl.ds(pl.multiple_of(chip * KT, KT), KT)

    def arrive(src):
        spot = pl.ds(pl.multiple_of(src * TOK, TOK), TOK)
        remote(kv8.at[0], kv_all.at[spot, :], kvs.at[0], kvr.at[src], x, y, 1 - c).wait_recv()

    def score(fresh, half, j, q2):
        chip, ds = keys_of(half, j)
        block = kv_all[ds, :]
        if fresh:
            vt_ref[0:64, ds] = block.T[64:128]
        return jnp.dot(block, q2, preferred_element_type=F32)

    def suffix_len(member):
        lane = lax.broadcasted_iota(jnp.int32, (1, 32), 1)
        request = jnp.sum(jnp.where(lane == member, assign_ref[...].astype(F32), 0.0), axis=1, keepdims=True)
        return jnp.sum(
            jnp.where(lane.astype(F32) == request, lengths_ref[...].astype(F32), 0.0), axis=1, keepdims=True
        )

    def begin(kth):
        tx = rem4(x + ORDER[kth])
        back = (4 - ORDER[kth]) % 4
        for i, (dx, dc) in enumerate(peers):
            if dx == back:
                x_copy(i).wait_recv()
        for j in range(2):
            blk = x_all[2 * tx + j]
            qt = (blk[:, 0:128].astype(F32) * ATTN_SCALE).astype(BF16).T
            q2 = jnp.concatenate([qt[0:64], qt[64:128]], axis=1)
            q2 = jnp.concatenate([q2, jnp.zeros((64, 512), BF16)], axis=0)
            skv = blk[:, 128:256]
            s = jnp.dot(skv, q2, preferred_element_type=F32)
            srow = lax.broadcasted_iota(jnp.int32, (TOK, 512), 0)
            tcol = lax.broadcasted_iota(jnp.int32, (TOK, 512), 1) & 255
            visible = (srow <= tcol) & (srow.astype(F32) < suffix_len(tx * 8 + y * 2 + j))
            s = jnp.where(visible, s * LOG2E, -jnp.inf)
            m = jnp.max(s, axis=0, keepdims=True)
            p = jnp.exp2(s - m)
            l = jnp.sum(p, axis=0, keepdims=True)
            acc = jnp.dot(skv.T[64:128], p.astype(BF16), preferred_element_type=F32)
            cols = slice(512 * j, 512 * (j + 1))
            q_st[kth, :, cols] = q2
            m_st[kth, :, cols] = m
            acc_st[kth, 0:64, cols] = acc
            acc_st[kth, 64:80, cols] = jnp.broadcast_to(l, (16, 512))

    def attend(kth, half, fresh):
        q2 = q_st[kth]
        lo, hi = half * HALF, half * HALF + HALF
        if fresh and half == 0:
            arrive(2 * (4 * x + y) + 1 - c)
        elif fresh:
            chip, ds = keys_of(half, jnp.int32(lo))
            arrive(2 * chip)
            arrive(2 * chip + 1)
        s_ref[0] = score(fresh, half, jnp.int32(lo), q2)

        def step(i, carry):
            m, acc = carry
            for u in range(2):
                kk = lo + 2 * i + u
                nxt = jnp.minimum(kk + 1, hi - 1)
                if fresh:

                    @pl.when(kk + 1 < hi)
                    def _():
                        chip, ds = keys_of(half, nxt)
                        arrive(2 * chip)
                        arrive(2 * chip + 1)

                s = s_ref[u]
                s_ref[1 - u] = score(fresh, half, nxt, q2)
                s = s * LOG2E
                mn = jnp.maximum(m, jnp.max(s, axis=0, keepdims=True))
                p = jnp.exp2(s - mn).astype(BF16)
                chip, ds = keys_of(half, kk)
                acc = acc * jnp.exp2(m - mn) + jnp.dot(vt_ref[:, ds], p, preferred_element_type=F32)
                m = mn
            return m, acc

        m, acc = lax.fori_loop(0, HALF // 2, step, (m_st[kth], acc_st[kth]))
        if half == 0:
            m_st[kth] = m
            acc_st[kth] = acc
            return
        tx = rem4(x + ORDER[kth])
        out = acc[0:64] / acc[64:65]
        for j in range(2):
            ot = out[:, 512 * j : 512 * (j + 1)].T.astype(BF16)
            part_ref[2 * tx + j] = jnp.concatenate([ot[0:256], ot[256:512]], axis=1)

    def ctx_copy(i):
        tx, tc = peer(i)
        return remote(part_ref.at[2 * tx + tc], ctx_all.at[pos], cs.at[i], cr.at[i], tx, y, tc)

    for kth in range(4):
        if kth == 2:
            column_start((0,))
            weights_start(1, (1, 2))
        if kth == 3:
            weights_start(0, (0,))
        begin(kth)
        attend(kth, 0, kth == 0)
    for kth in (3, 1, 2, 0):
        if kth == 2:
            column_start((1, 2))
            weights_start(0, (1, 2))
        attend(kth, 1, kth == 3)
        if kth == 0:
            ctx_all[pos] = part_ref[pos]
        for i, (dx, dc) in enumerate(peers):
            if dx == ORDER[kth]:
                ctx_copy(i).start()

    for i in range(7):
        ctx_copy(i).wait_recv()
    ctx = jnp.concatenate([ctx_all[h] for h in range(8)], axis=1)
    context_ref[...] = ctx
    projected = jnp.dot(ctx, wo_ref[...], preferred_element_type=F32)
    hidden = (tok_ref[...].astype(F32) + RESIDUAL_SCALE * projected).astype(BF16)
    hidden_ref[...] = hidden
    wide = hidden.astype(F32)
    mean_square = jnp.mean(wide * wide, axis=-1, keepdims=True)
    moe_buf[...] = (wide * lax.rsqrt(mean_square + NORM_EPS) * mgain_ref[...]).astype(BF16)

    def moe_copy(i, dx):
        return remote(moe_buf, moe_all.at[pos], ms.at[i], mr.at[i], rem4(x + dx), y, c)

    def relay_copy(i, spot, src):
        return remote(src, moe_all.at[spot], ms.at[3 + i], mr.at[3 + i], x, y, 1 - c)

    keep = pltpu.make_async_copy(moe_buf, moe_all.at[pos], own_sem.at[2])
    for i, dx in enumerate((1, 3, 2)):
        moe_copy(i, dx).start()
    relay_copy(3, pos, moe_buf).start()
    keep.start()
    relays = []
    for i, dx in enumerate((1, 3, 2)):
        moe_copy(i, dx).wait_recv()
        spot = 2 * rem4(x - dx) + c
        cp = relay_copy(i, spot, moe_all.at[spot])
        cp.start()
        relays.append(cp)

    keep.wait()
    for cp in own_copies():
        cp.wait()
    for i, dx in enumerate((1, 3, 2)):
        moe_copy(i, dx).wait_send()
    for cp in relays + [relay_copy(3, pos, moe_buf)]:
        cp.wait()
    for i in range(7):
        x_copy(i).wait_send()
        ctx_copy(i).wait_send()
        for cp in table_copies(i):
            cp.wait()
    for half in (0, 1):
        kv_each(half, lambda cp: cp.wait_send())
    for dy in (1, 3, 2):
        for cp in weight_copies(dy, 1):
            cp.wait_send()
        for cp in weight_copies(dy, 0):
            cp.wait()
    for slot in range(3):
        for dz in (1, 3, 2):
            for cp in column_copies(dz, slot):
                cp.wait()


def front(*args):
    anywhere = pl.BlockSpec(memory_space=pl.ANY)
    dma = pltpu.SemaphoreType.DMA
    shape = jax.ShapeDtypeStruct
    return pl.pallas_call(
        front_kernel,
        out_shape=(
            shape((TOK, D), BF16), shape((TOK, D), BF16), shape((8, TOK, D), BF16),
            shape((8, 8, TOK), jnp.int32), shape((8, 8, TOK), F32),
            shape((3, D, FF), BF16), shape((3, D, FF), BF16), shape((3, FF, D), BF16),
        ),
        in_specs=vmem_specs(13) + [anywhere] * 5,
        out_specs=tuple(vmem_specs(2) + [anywhere] * 6),
        scratch_shapes=[
            pltpu.VMEM((8, TOK, 128), BF16),
            pltpu.VMEM((PREFIX, 128), BF16),
            pltpu.VMEM((8, TOK, 256), BF16),
            pltpu.VMEM((8, TOK, 256), BF16),
            pltpu.VMEM((80, PREFIX), BF16),
            pltpu.VMEM((2, KT, 1024), F32),
            pltpu.VMEM((4, 128, 1024), BF16),
            pltpu.VMEM((4, 1, 1024), F32),
            pltpu.VMEM((4, 80, 1024), F32),
            pltpu.VMEM((8, TOK, 128), BF16),
            pltpu.VMEM((8, TOK, 128), BF16),
            pltpu.VMEM((TOK, D), BF16),
            dma((32,)), dma((32,)), dma((7,)), dma((7,)), dma((7,)), dma((7,)), dma((7,)), dma((7,)),
            dma((2, 7)), dma((2, 7)), dma((3, 3)), dma((3, 3)), dma((3, 3)), dma((3, 3)),
            dma((3, 3, 3)), dma((3, 3, 3)), dma((3,)),
        ],
        compiler_params=pltpu.CompilerParams(
            vmem_limit_bytes=VMEM_BYTES, collective_id=0, has_side_effects=True
        ),
        name="front",
    )(*args)


PHASES = (2, 1, 3, 0)


def tail_kernel(
    moe_all, ids_ref, rw_ref, g_in, u_in, d_in, g_all, u_all, d_all, mix_ref,
    x_v, g_v, u_v, d_v, rank_ref, wt_ref, rows_ref, eo_ref, pw_ref, keep_ref,
    pair_send, pair_recv, out_send, out_recv, xsem, wsem, ps, pr, os, orr,
):
    grp = lax.axis_index("grp")
    me = lax.axis_index("req")
    x, y, c = lax.div(me, 8), lax.rem(lax.div(me, 2), 4), lax.rem(me, 2)

    def remote(src, dst, send, recv, tx, tc):
        return pltpu.make_async_remote_copy(
            src_ref=src, dst_ref=dst, send_sem=send, recv_sem=recv,
            device_id=(grp, tx * 8 + y * 2 + tc), device_id_type=MESH_ID,
        )

    barrier = pltpu.get_barrier_semaphore()
    for tx, tc in [(x, 1 - c)] + [(rem4(x + dx), c) for dx in (1, 2, 3)]:
        pl.semaphore_signal(barrier, inc=1, device_id=(grp, tx * 8 + y * 2 + tc), device_id_type=MESH_ID)

    def two(k):
        return pl.ds(2 * rem4(x + PHASES[k]), 2)

    def load_rows(k):
        return pltpu.make_async_copy(moe_all.at[two(k)], x_v.at[k], xsem.at[k])

    def load_weights(e, own=False):
        sources = (g_in, u_in, d_in) if own else (g_all, u_all, d_all)
        return [
            pltpu.make_async_copy(src.at[0 if own else e], dst.at[e], wsem.at[t, e])
            for t, (src, dst) in enumerate(zip(sources, (g_v, u_v, d_v)))
        ]

    load_rows(0).start()
    for e in range(4):
        for cp in load_weights(e, e == 3):
            cp.start()
        if e < 3:
            load_rows(e + 1).start()

    tri = (
        lax.broadcasted_iota(jnp.int32, (TOK, TOK), 0) < lax.broadcasted_iota(jnp.int32, (TOK, TOK), 1)
    ).astype(BF16)
    for b in range(8):
        masks, weights = [], []
        for e in range(4):
            hits = ids_ref[b] == x * 8 + rem4(y + 1 + e) * 2 + c
            masks.append(jnp.max(hits.astype(F32), axis=0, keepdims=True))
            weights.append(jnp.sum(jnp.where(hits, rw_ref[b], 0.0), axis=0, keepdims=True))
        mask = jnp.concatenate(masks + [jnp.zeros((12, TOK), F32)], axis=0)
        rank = jnp.dot(mask.astype(BF16), tri, preferred_element_type=F32)
        rank_ref[b] = jnp.where(mask > 0, rank, -1.0)[0:8]
        wt_ref[b] = jnp.concatenate(weights + [jnp.zeros((4, TOK), F32)], axis=0)
    slot = lax.broadcasted_iota(jnp.int32, (CAP, TOK), 0).astype(F32)
    pl.semaphore_wait(barrier, 4)

    def pair_copy(k):
        return remote(pair_send.at[k], pair_recv.at[k], ps.at[k], pr.at[k], x, 1 - c)

    def out_copy(k):
        return remote(out_send.at[k], out_recv.at[k], os.at[k], orr.at[k], rem4(x + PHASES[k]), c)

    def finish(k):
        pair_copy(k).wait_recv()
        total = keep_ref[k % 2] + pair_recv[k].astype(F32)
        if k < 3:
            out_send[k] = total.astype(BF16)
            out_copy(k).start()
        return total

    for k in range(4):
        base = 2 * rem4(x + PHASES[k])
        load_rows(k).wait()

        def expert(e, carry):
            if k == 0:
                for src, dst, t in ((g_in, g_v, 0), (u_in, u_v, 1), (d_in, d_v, 2)):
                    pltpu.make_async_copy(src.at[0], dst.at[e], wsem.at[t, e]).wait()
            here = pl.ds(pl.multiple_of(e * CAP, CAP), CAP)
            for j in range(2):
                chosen = slot == rank_ref[base + j, pl.ds(e, 1), :]
                rows_ref[j * CAP : (j + 1) * CAP] = jnp.dot(
                    chosen.astype(BF16), x_v[k, j], preferred_element_type=F32
                ).astype(BF16)
                pw_ref[j, here] = jnp.where(chosen, wt_ref[base + j, pl.ds(e, 1), :], 0.0).astype(BF16)
            rows = rows_ref[...]
            gate = jnp.dot(rows, g_v[e], preferred_element_type=F32)
            up = jnp.dot(rows, u_v[e], preferred_element_type=F32)
            act = (jax.nn.silu(gate) * up).astype(BF16)
            out = jnp.dot(act, d_v[e], preferred_element_type=F32).astype(BF16)
            for j in range(2):
                eo_ref[j, here] = out[j * CAP : (j + 1) * CAP]
            if k > 0:

                @pl.when(e == 1)
                def _():
                    finish(k - 1)

            return carry

        lax.fori_loop(0, 4, expert, 0)

        def combine(j):
            return lax.dot_general(pw_ref[j], eo_ref[j], (((0,), (0,)), ((), ())), preferred_element_type=F32)

        pair_send[k] = combine(1 - c).astype(BF16)
        pair_copy(k).start()
        keep_ref[k % 2] = combine(c)
    total = finish(3)
    for k in range(3):
        out_copy(k).wait_recv()
        total = total + out_recv[k].astype(F32)
    mix_ref[...] = total.astype(BF16)
    for k in range(4):
        pair_copy(k).wait_send()
    for k in range(3):
        out_copy(k).wait_send()


def tail(moe_all, ids, rw, own, gathered):
    anywhere = pl.BlockSpec(memory_space=pl.ANY)
    dma = pltpu.SemaphoreType.DMA
    return pl.pallas_call(
        tail_kernel,
        out_shape=jax.ShapeDtypeStruct((TOK, D), BF16),
        in_specs=[anywhere] + vmem_specs(2) + [anywhere] * 6,
        out_specs=vmem_specs(1)[0],
        scratch_shapes=[
            pltpu.VMEM((4, 2, TOK, D), BF16),
            pltpu.VMEM((4, D, FF), BF16),
            pltpu.VMEM((4, D, FF), BF16),
            pltpu.VMEM((4, FF, D), BF16),
            pltpu.VMEM((8, 8, TOK), F32),
            pltpu.VMEM((8, 8, TOK), F32),
            pltpu.VMEM((2 * CAP, D), BF16),
            pltpu.VMEM((2, 4 * CAP, D), BF16),
            pltpu.VMEM((2, 4 * CAP, TOK), BF16),
            pltpu.VMEM((2, TOK, D), F32),
            pltpu.VMEM((4, TOK, D), BF16),
            pltpu.VMEM((4, TOK, D), BF16),
            pltpu.VMEM((3, TOK, D), BF16),
            pltpu.VMEM((3, TOK, D), BF16),
            dma((4,)), dma((3, 4)), dma((4,)), dma((4,)), dma((3,)), dma((3,)),
        ],
        compiler_params=pltpu.CompilerParams(
            vmem_limit_bytes=VMEM_BYTES, collective_id=1, has_side_effects=True
        ),
        name="tail",
    )(moe_all, ids, rw, *own, *gathered)


def local(
    tokens, attn_gain, w_query, w_key, w_value, w_out, prefix_keys, prefix_values,
    lengths, assignment, moe_gain, expert_ids, route_weights, w_gate, w_up, w_down,
):
    cos, sin = rope_tables()
    context, hidden, moe_all, ids, rw, wg, wu, wd = front(
        tokens[0], attn_gain[None], w_query, w_key, w_value, w_out, moe_gain[None], cos, sin,
        prefix_keys[0], prefix_values[0], assignment, lengths, expert_ids[0].T, route_weights[0].T, w_gate, w_up, w_down,
    )
    expert_mix = tail(moe_all, ids, rw, (w_gate, w_up, w_down), (wg, wu, wd))
    return (context[None], hidden[None], expert_mix[None])


def solution(mesh):
    placed = (
        P("grp", "req", None), P(), P(), P(), P(), P(),
        P("grp", "req", None), P("grp", "req", None), P("grp", None), P("grp", None),
        P(), P("grp", "req", None), P("grp", "req", None),
        P("req", None, None), P("req", None, None), P("req", None, None),
    )
    return jax.shard_map(
        local,
        mesh=mesh,
        in_specs=placed,
        out_specs=(P("grp", "req", None), P("grp", "req", None), P("grp", "req", None)),
        check_vma=False,
    )
```

```python
import functools

import jax
import jax.numpy as jnp
import numpy as np
from jax import lax
from jax.experimental import pallas as pl
from jax.experimental.pallas import tpu as pltpu
from jax.sharding import PartitionSpec as P

HD = 64
CAP = 96
PREFIX = 8192
TOK = 256
D = 1024
FF = 512
NORM_EPS = 1e-06
ATTN_SCALE = 0.015625
RESIDUAL_SCALE = 0.22
ROPE_BASE = 10000.0
LOG2E = 1.4426950408889634
VMEM_BYTES = 60000 * 1024
BF16 = jnp.bfloat16
F32 = jnp.float32


def rope_tables():
    half = HD // 2
    freq = np.float32(ROPE_BASE) ** (-(np.arange(half, dtype=np.float32) * 2.0 / HD))
    pos = (PREFIX + np.arange(TOK)).astype(np.float32)
    angles = (pos[:, None] * freq.astype(np.float32)[None, :]).astype(np.float64)
    cos, sin = np.cos(angles), np.sin(angles)
    cos128 = np.concatenate([cos] * 4, axis=1).astype(np.float32)
    sin128 = np.concatenate([-sin, sin, -sin, sin], axis=1).astype(np.float32)
    return cos128, sin128


def vmem_specs(n):
    return [pl.BlockSpec(memory_space=pltpu.VMEM)] * n


def params():
    return pltpu.CompilerParams(vmem_limit_bytes=VMEM_BYTES)


MESH_ID = pl.DeviceIdType.MESH
KT = 512
ORDER = (0, 1, 3, 2)
HALF = 8
WIDE = ((384, 160), (384, 160), (192, 80))


def rem4(v):
    return lax.rem(v + 4, 4)


def front_kernel(
    tok_ref, again_ref, wq_ref, wk_ref, wv_ref, wo_ref, mgain_ref, cos_ref, sin_ref, pk_ref, pv_ref, assign_ref, lengths_ref,
    ids_in, rw_in, g_in, u_in, d_in,
    context_ref, hidden_ref, moe_all, ids_all, rw_all, g_all, u_all, d_all,
    kv8, kv_all, x_send, x_all, vt_ref, s_ref, q_st, m_st, acc_st, part_ref, ctx_all, moe_buf,
    kvs, kvr, xs, xr, cs, cr, ms, mr, ts, tr, ws, wr, vs, vr, zs, zr, own_sem,
):
    grp = lax.axis_index("grp")
    me = lax.axis_index("req")
    x, y, c = lax.div(me, 8), lax.rem(lax.div(me, 2), 4), lax.rem(me, 2)
    pos = 2 * x + c

    def remote(src, dst, send, recv, tx, ty, tc, tg=None):
        where = (grp if tg is None else tg, tx * 8 + ty * 2 + tc)
        return pltpu.make_async_remote_copy(
            src_ref=src, dst_ref=dst, send_sem=send, recv_sem=recv, device_id=where, device_id_type=MESH_ID
        )

    barrier = pltpu.get_barrier_semaphore()

    def greet(i, carry):
        pl.semaphore_signal(barrier, inc=1, device_id=(grp, lax.rem(me + i, 32)), device_id_type=MESH_ID)
        return carry

    lax.fori_loop(1, 32, greet, 0)
    for dz in (1, 2, 3):
        pl.semaphore_signal(barrier, inc=1, device_id=(rem4(grp + dz), me), device_id_type=MESH_ID)

    def own_copies():
        pairs = [(ids_in, ids_all.at[pos]), (rw_in, rw_all.at[pos])]
        return [pltpu.make_async_copy(a, b, own_sem.at[i]) for i, (a, b) in enumerate(pairs)]

    for cp in own_copies():
        cp.start()

    for pair in range(4):
        kr = pk_ref[:, 128 * pair : 128 * pair + 128]
        vr_ = pv_ref[:, 128 * pair : 128 * pair + 128]
        kv8[2 * pair] = jnp.concatenate([kr[:, 0:64], vr_[:, 0:64]], axis=1)
        kv8[2 * pair + 1] = jnp.concatenate([kr[:, 64:128], vr_[:, 64:128]], axis=1)
    mine = pl.ds(pl.multiple_of(me * TOK, TOK), TOK)
    kv_all[mine, :] = kv8[pos]
    pl.semaphore_wait(barrier, 34)

    def offset(half, j):
        t, u = lax.div(j, 4) - 2 * half, lax.rem(j, 4)
        side = 1 + 2 * lax.div(u, 2)
        if half == 0:
            dx = t * side
            return dx, (1 - t) * u + t * lax.rem(u, 2) * dx
        return (1 - t) * side + 2 * t, (1 - t) * (2 + lax.rem(u, 2) * (2 - side)) + t * u

    def kv_copy(half, j, tc):
        dx, dy = offset(half, j)
        tx, ty = lax.rem(x + dx, 4), lax.rem(y + dy, 4)
        return remote(kv8.at[2 * tx + tc], kv_all.at[mine, :], kvs.at[2 * j + tc], kvr.at[me], tx, ty, tc)

    def kv_each(half, what):
        def both(j, carry):
            for tc in (0, 1):
                what(kv_copy(half, j, tc))
            return carry

        if half == 0:
            what(remote(kv8.at[2 * x + 1 - c], kv_all.at[mine, :], kvs.at[0], kvr.at[me], x, y, 1 - c))
        lax.fori_loop(1 if half == 0 else HALF, HALF if half == 0 else 2 * HALF, both, 0)

    kv_each(0, lambda cp: cp.start())

    peers = [(0, 1)] + [(dx, dc) for dx in (1, 3, 2) for dc in (0, 1)]

    def peer(i):
        dx, dc = peers[i]
        return rem4(x + dx), lax.rem(c + dc, 2)

    def table_copies(i):
        tx, tc = peer(i)
        return (
            remote(ids_in, ids_all.at[pos], ts.at[0, i], tr.at[0, i], tx, y, tc),
            remote(rw_in, rw_all.at[pos], ts.at[1, i], tr.at[1, i], tx, y, tc),
        )

    for i in range(7):
        for cp in table_copies(i):
            cp.start()

    stacks = ((g_in, g_all), (u_in, u_all), (d_in, d_all))

    def quarter_rows(t):
        straight, quarter = WIDE[t]
        return pl.ds(pl.multiple_of(straight + grp * quarter, 16), quarter)

    def weight_copies(dy, part, only=(0, 1, 2)):
        out = []
        for t in only:
            src, dst = stacks[t]
            rows = quarter_rows(t) if part else pl.ds(0, WIDE[t][0])
            sems = (vs, vr) if part else (ws, wr)
            out.append(
                remote(src.at[0, rows, :], dst.at[3 - dy, rows, :], sems[0].at[dy - 1, t], sems[1].at[dy - 1, t],
                       x, rem4(y + dy), c)
            )
        return out

    def column_copies(dz, slot, only=(0, 1, 2)):
        out = []
        for t in only:
            src, dst = stacks[t]
            rows = quarter_rows(t)
            out.append(
                remote(dst.at[slot, rows, :], dst.at[slot, rows, :], zs.at[dz - 1, slot, t], zr.at[dz - 1, slot, t],
                       x, y, c, rem4(grp + dz))
            )
        return out

    def weights_start(part, only):
        for dy in (1, 3, 2):
            for cp in weight_copies(dy, part, only):
                cp.start()

    def column_start(only):
        for dy in (1, 3, 2):
            for cp in weight_copies(dy, 1, only):
                cp.wait_recv()
        for slot in range(3):
            for dz in (1, 3, 2):
                for cp in column_copies(dz, slot, only):
                    cp.start()

    weights_start(1, (0,))

    rows = tok_ref[...].astype(F32)
    mean_square = jnp.mean(rows * rows, axis=-1, keepdims=True)
    normed = (rows * lax.rsqrt(mean_square + NORM_EPS) * again_ref[...]).astype(BF16)
    cos, sin = cos_ref[...], sin_ref[...]
    low = (lax.broadcasted_iota(jnp.int32, (TOK, 128), 1) & 32) == 0

    def rotate(part):
        other = jnp.where(low, pltpu.roll(part, 96, 1), pltpu.roll(part, 32, 1))
        return (part * cos + other * sin).astype(BF16)

    q = jnp.dot(normed, wq_ref[...], preferred_element_type=F32)
    k = jnp.dot(normed, wk_ref[...], preferred_element_type=F32)
    v = jnp.dot(normed, wv_ref[...], preferred_element_type=F32).astype(BF16)
    for h in range(8):
        x_send[h, :, 0:128] = rotate(q[:, 128 * h : 128 * h + 128])
    for pair in range(4):
        kr = rotate(k[:, 128 * pair : 128 * pair + 128])
        vr_ = v[:, 128 * pair : 128 * pair + 128]
        x_send[2 * pair, :, 128:256] = jnp.concatenate([kr[:, 0:64], vr_[:, 0:64]], axis=1)
        x_send[2 * pair + 1, :, 128:256] = jnp.concatenate([kr[:, 64:128], vr_[:, 64:128]], axis=1)
    x_all[pos] = x_send[pos]

    def x_copy(i):
        tx, tc = peer(i)
        return remote(x_send.at[2 * tx + tc], x_all.at[pos], xs.at[i], xr.at[i], tx, y, tc)

    for i in range(7):
        x_copy(i).start()
    kv_each(1, lambda cp: cp.start())
    vt_ref[64:80, :] = jnp.ones((16, PREFIX), BF16)

    def keys_of(half, j):
        dx, dy = offset(half, j)
        chip = lax.rem(x + 4 - dx, 4) * 4 + lax.rem(y + 4 - dy, 4)
        return chip, pl.ds(pl.multiple_of(chip * KT, KT), KT)

    def arrive(src):
        spot = pl.ds(pl.multiple_of(src * TOK, TOK), TOK)
        remote(kv8.at[0], kv_all.at[spot, :], kvs.at[0], kvr.at[src], x, y, 1 - c).wait_recv()

    def score(fresh, half, j, q2):
        chip, ds = keys_of(half, j)
        block = kv_all[ds, :]
        if fresh:
            vt_ref[0:64, ds] = block.T[64:128]
        return jnp.dot(block, q2, preferred_element_type=F32)

    def suffix_len(member):
        lane = lax.broadcasted_iota(jnp.int32, (1, 32), 1)
        request = jnp.sum(jnp.where(lane == member, assign_ref[...].astype(F32), 0.0), axis=1, keepdims=True)
        return jnp.sum(
            jnp.where(lane.astype(F32) == request, lengths_ref[...].astype(F32), 0.0), axis=1, keepdims=True
        )

    def begin(kth):
        tx = rem4(x + ORDER[kth])
        back = (4 - ORDER[kth]) % 4
        for i, (dx, dc) in enumerate(peers):
            if dx == back:
                x_copy(i).wait_recv()
        for j in range(2):
            blk = x_all[2 * tx + j]
            qt = (blk[:, 0:128].astype(F32) * ATTN_SCALE).astype(BF16).T
            q2 = jnp.concatenate([qt[0:64], qt[64:128]], axis=1)
            q2 = jnp.concatenate([q2, jnp.zeros((64, 512), BF16)], axis=0)
            skv = blk[:, 128:256]
            s = jnp.dot(skv, q2, preferred_element_type=F32)
            srow = lax.broadcasted_iota(jnp.int32, (TOK, 512), 0)
            tcol = lax.broadcasted_iota(jnp.int32, (TOK, 512), 1) & 255
            visible = (srow <= tcol) & (srow.astype(F32) < suffix_len(tx * 8 + y * 2 + j))
            s = jnp.where(visible, s * LOG2E, -jnp.inf)
            m = jnp.max(s, axis=0, keepdims=True)
            p = jnp.exp2(s - m)
            l = jnp.sum(p, axis=0, keepdims=True)
            acc = jnp.dot(skv.T[64:128], p.astype(BF16), preferred_element_type=F32)
            cols = slice(512 * j, 512 * (j + 1))
            q_st[kth, :, cols] = q2
            m_st[kth, :, cols] = m
            acc_st[kth, 0:64, cols] = acc
            acc_st[kth, 64:80, cols] = jnp.broadcast_to(l, (16, 512))

    def attend(kth, half, fresh):
        q2 = q_st[kth]
        lo, hi = half * HALF, half * HALF + HALF
        if fresh and half == 0:
            arrive(2 * (4 * x + y) + 1 - c)
        elif fresh:
            chip, ds = keys_of(half, jnp.int32(lo))
            arrive(2 * chip)
            arrive(2 * chip + 1)
        s_ref[0] = score(fresh, half, jnp.int32(lo), q2)

        def step(i, carry):
            m, acc = carry
            for u in range(2):
                kk = lo + 2 * i + u
                nxt = jnp.minimum(kk + 1, hi - 1)
                if fresh:

                    @pl.when(kk + 1 < hi)
                    def _():
                        chip, ds = keys_of(half, nxt)
                        arrive(2 * chip)
                        arrive(2 * chip + 1)

                s = s_ref[u]
                s_ref[1 - u] = score(fresh, half, nxt, q2)
                s = s * LOG2E
                mn = jnp.maximum(m, jnp.max(s, axis=0, keepdims=True))
                p = jnp.exp2(s - mn).astype(BF16)
                chip, ds = keys_of(half, kk)
                acc = acc * jnp.exp2(m - mn) + jnp.dot(vt_ref[:, ds], p, preferred_element_type=F32)
                m = mn
            return m, acc

        m, acc = lax.fori_loop(0, HALF // 2, step, (m_st[kth], acc_st[kth]))
        if half == 0:
            m_st[kth] = m
            acc_st[kth] = acc
            return
        tx = rem4(x + ORDER[kth])
        out = acc[0:64] / acc[64:65]
        for j in range(2):
            ot = out[:, 512 * j : 512 * (j + 1)].T.astype(BF16)
            part_ref[2 * tx + j] = jnp.concatenate([ot[0:256], ot[256:512]], axis=1)

    def ctx_copy(i):
        tx, tc = peer(i)
        return remote(part_ref.at[2 * tx + tc], ctx_all.at[pos], cs.at[i], cr.at[i], tx, y, tc)

    for kth in range(4):
        if kth == 2:
            column_start((0,))
            weights_start(1, (1, 2))
        if kth == 3:
            weights_start(0, (0,))
        begin(kth)
        attend(kth, 0, kth == 0)
    for kth in (3, 1, 2, 0):
        if kth == 2:
            column_start((1, 2))
            weights_start(0, (1, 2))
        attend(kth, 1, kth == 3)
        if kth == 0:
            ctx_all[pos] = part_ref[pos]
        for i, (dx, dc) in enumerate(peers):
            if dx == ORDER[kth]:
                ctx_copy(i).start()

    for i in range(7):
        ctx_copy(i).wait_recv()
    ctx = jnp.concatenate([ctx_all[h] for h in range(8)], axis=1)
    context_ref[...] = ctx
    projected = jnp.dot(ctx, wo_ref[...], preferred_element_type=F32)
    hidden = (tok_ref[...].astype(F32) + RESIDUAL_SCALE * projected).astype(BF16)
    hidden_ref[...] = hidden
    wide = hidden.astype(F32)
    mean_square = jnp.mean(wide * wide, axis=-1, keepdims=True)
    moe_buf[...] = (wide * lax.rsqrt(mean_square + NORM_EPS) * mgain_ref[...]).astype(BF16)

    def moe_copy(i, dx):
        return remote(moe_buf, moe_all.at[pos], ms.at[i], mr.at[i], rem4(x + dx), y, c)

    def onward_copy(i):
        step = 1 - 2 * i
        rows = pl.ds(TOK // 2 * i, TOK // 2)
        block = moe_all.at[2 * rem4(x - step) + c, rows, :]
        return remote(block, block, ms.at[2 + i], mr.at[2 + i], rem4(x + step), y, c)

    def relay_copy(i, spot, src):
        return remote(src, moe_all.at[spot], ms.at[4 + i], mr.at[4 + i], x, y, 1 - c)

    keep = pltpu.make_async_copy(moe_buf, moe_all.at[pos], own_sem.at[2])
    for i, dx in enumerate((1, 3)):
        moe_copy(i, dx).start()
    relays = [relay_copy(3, pos, moe_buf)]
    relays[0].start()
    keep.start()
    for i, dx in enumerate((1, 3)):
        moe_copy(i, dx).wait_recv()
        onward_copy(i).start()
        spot = 2 * rem4(x - dx) + c
        relays.append(relay_copy(i, spot, moe_all.at[spot]))
        relays[-1].start()
    for i in range(2):
        onward_copy(i).wait_recv()
    spot = 2 * rem4(x + 2) + c
    relays.append(relay_copy(2, spot, moe_all.at[spot]))
    relays[-1].start()

    keep.wait()
    for cp in own_copies():
        cp.wait()
    for i, dx in enumerate((1, 3)):
        moe_copy(i, dx).wait_send()
        onward_copy(i).wait_send()
    for cp in relays:
        cp.wait()
    for i in range(7):
        x_copy(i).wait_send()
        ctx_copy(i).wait_send()
        for cp in table_copies(i):
            cp.wait()
    for half in (0, 1):
        kv_each(half, lambda cp: cp.wait_send())
    for dy in (1, 3, 2):
        for cp in weight_copies(dy, 1):
            cp.wait_send()
        for cp in weight_copies(dy, 0):
            cp.wait()
    for slot in range(3):
        for dz in (1, 3, 2):
            for cp in column_copies(dz, slot):
                cp.wait()


def front(*args):
    anywhere = pl.BlockSpec(memory_space=pl.ANY)
    dma = pltpu.SemaphoreType.DMA
    shape = jax.ShapeDtypeStruct
    return pl.pallas_call(
        front_kernel,
        out_shape=(
            shape((TOK, D), BF16), shape((TOK, D), BF16), shape((8, TOK, D), BF16),
            shape((8, 8, TOK), jnp.int32), shape((8, 8, TOK), F32),
            shape((3, D, FF), BF16), shape((3, D, FF), BF16), shape((3, FF, D), BF16),
        ),
        in_specs=vmem_specs(13) + [anywhere] * 5,
        out_specs=tuple(vmem_specs(2) + [anywhere] * 6),
        scratch_shapes=[
            pltpu.VMEM((8, TOK, 128), BF16),
            pltpu.VMEM((PREFIX, 128), BF16),
            pltpu.VMEM((8, TOK, 256), BF16),
            pltpu.VMEM((8, TOK, 256), BF16),
            pltpu.VMEM((80, PREFIX), BF16),
            pltpu.VMEM((2, KT, 1024), F32),
            pltpu.VMEM((4, 128, 1024), BF16),
            pltpu.VMEM((4, 1, 1024), F32),
            pltpu.VMEM((4, 80, 1024), F32),
            pltpu.VMEM((8, TOK, 128), BF16),
            pltpu.VMEM((8, TOK, 128), BF16),
            pltpu.VMEM((TOK, D), BF16),
            dma((32,)), dma((32,)), dma((7,)), dma((7,)), dma((7,)), dma((7,)), dma((8,)), dma((8,)),
            dma((2, 7)), dma((2, 7)), dma((3, 3)), dma((3, 3)), dma((3, 3)), dma((3, 3)),
            dma((3, 3, 3)), dma((3, 3, 3)), dma((3,)),
        ],
        compiler_params=pltpu.CompilerParams(
            vmem_limit_bytes=VMEM_BYTES, collective_id=0, has_side_effects=True
        ),
        name="front",
    )(*args)


PHASES = (2, 1, 3, 0)


def tail_kernel(
    moe_all, ids_ref, rw_ref, g_in, u_in, d_in, g_all, u_all, d_all, total_ref, out_recv,
    x_v, g_v, u_v, d_v, rank_ref, wt_ref, rows_ref, eo_ref, pw_ref, keep_ref,
    pair_send, pair_recv, out_send, xsem, wsem, ps, pr, os, orr,
):
    grp = lax.axis_index("grp")
    me = lax.axis_index("req")
    x, y, c = lax.div(me, 8), lax.rem(lax.div(me, 2), 4), lax.rem(me, 2)

    def remote(src, dst, send, recv, tx, tc):
        return pltpu.make_async_remote_copy(
            src_ref=src, dst_ref=dst, send_sem=send, recv_sem=recv,
            device_id=(grp, tx * 8 + y * 2 + tc), device_id_type=MESH_ID,
        )

    barrier = pltpu.get_barrier_semaphore()
    for tx, tc in [(x, 1 - c)] + [(rem4(x + dx), c) for dx in (1, 2, 3)]:
        pl.semaphore_signal(barrier, inc=1, device_id=(grp, tx * 8 + y * 2 + tc), device_id_type=MESH_ID)

    def two(k):
        return pl.ds(2 * rem4(x + PHASES[k]), 2)

    def load_rows(k):
        return pltpu.make_async_copy(moe_all.at[two(k)], x_v.at[k], xsem.at[k])

    def load_weights(e, own=False):
        sources = (g_in, u_in, d_in) if own else (g_all, u_all, d_all)
        return [
            pltpu.make_async_copy(src.at[0 if own else e], dst.at[e], wsem.at[t, e])
            for t, (src, dst) in enumerate(zip(sources, (g_v, u_v, d_v)))
        ]

    load_rows(0).start()
    for e in range(4):
        for cp in load_weights(e, e == 3):
            cp.start()
        if e < 3:
            load_rows(e + 1).start()

    tri = (
        lax.broadcasted_iota(jnp.int32, (TOK, TOK), 0) < lax.broadcasted_iota(jnp.int32, (TOK, TOK), 1)
    ).astype(BF16)
    for b in range(8):
        masks, weights = [], []
        for e in range(4):
            hits = ids_ref[b] == x * 8 + rem4(y + 1 + e) * 2 + c
            masks.append(jnp.max(hits.astype(F32), axis=0, keepdims=True))
            weights.append(jnp.sum(jnp.where(hits, rw_ref[b], 0.0), axis=0, keepdims=True))
        mask = jnp.concatenate(masks + [jnp.zeros((12, TOK), F32)], axis=0)
        rank = jnp.dot(mask.astype(BF16), tri, preferred_element_type=F32)
        rank_ref[b] = jnp.where(mask > 0, rank, -1.0)[0:8]
        wt_ref[b] = jnp.concatenate(weights + [jnp.zeros((4, TOK), F32)], axis=0)
    slot = lax.broadcasted_iota(jnp.int32, (CAP, TOK), 0).astype(F32)
    pl.semaphore_wait(barrier, 4)

    def pair_copy(k):
        return remote(pair_send.at[k], pair_recv.at[k], ps.at[k], pr.at[k], x, 1 - c)

    def out_copy(k):
        return remote(out_send.at[k], out_recv.at[k], os.at[k], orr.at[k], rem4(x + PHASES[k]), c)

    def finish(k):
        pair_copy(k).wait_recv()
        total = keep_ref[k % 2] + pair_recv[k].astype(F32)
        if k < 3:
            out_send[k] = total.astype(BF16)
            out_copy(k).start()
        return total

    for k in range(4):
        base = 2 * rem4(x + PHASES[k])
        load_rows(k).wait()

        def expert(e, carry):
            if k == 0:
                for src, dst, t in ((g_in, g_v, 0), (u_in, u_v, 1), (d_in, d_v, 2)):
                    pltpu.make_async_copy(src.at[0], dst.at[e], wsem.at[t, e]).wait()
            here = pl.ds(pl.multiple_of(e * CAP, CAP), CAP)
            for j in range(2):
                chosen = slot == rank_ref[base + j, pl.ds(e, 1), :]
                rows_ref[j * CAP : (j + 1) * CAP] = jnp.dot(
                    chosen.astype(BF16), x_v[k, j], preferred_element_type=F32
                ).astype(BF16)
                pw_ref[j, here] = jnp.where(chosen, wt_ref[base + j, pl.ds(e, 1), :], 0.0).astype(BF16)
            rows = rows_ref[...]
            gate = jnp.dot(rows, g_v[e], preferred_element_type=F32)
            up = jnp.dot(rows, u_v[e], preferred_element_type=F32)
            act = (jax.nn.silu(gate) * up).astype(BF16)
            out = jnp.dot(act, d_v[e], preferred_element_type=F32).astype(BF16)
            for j in range(2):
                eo_ref[j, here] = out[j * CAP : (j + 1) * CAP]
            if k > 0:

                @pl.when(e == 0)
                def _():
                    finish(k - 1)

            return carry

        lax.fori_loop(0, 4, expert, 0)

        def combine(j):
            return lax.dot_general(pw_ref[j], eo_ref[j], (((0,), (0,)), ((), ())), preferred_element_type=F32)

        pair_send[k] = combine(1 - c).astype(BF16)
        pair_copy(k).start()
        keep_ref[k % 2] = combine(c)
    total_ref[...] = finish(3)
    for k in range(3):
        out_copy(k).wait_recv()
    for k in range(4):
        pair_copy(k).wait_send()
    for k in range(3):
        out_copy(k).wait_send()


def tail(moe_all, ids, rw, own, gathered):
    anywhere = pl.BlockSpec(memory_space=pl.ANY)
    dma = pltpu.SemaphoreType.DMA
    return pl.pallas_call(
        tail_kernel,
        out_shape=(jax.ShapeDtypeStruct((TOK, D), F32), jax.ShapeDtypeStruct((3, TOK, D), BF16)),
        in_specs=[anywhere] + vmem_specs(2) + [anywhere] * 6,
        out_specs=(vmem_specs(1)[0], anywhere),
        scratch_shapes=[
            pltpu.VMEM((4, 2, TOK, D), BF16),
            pltpu.VMEM((4, D, FF), BF16),
            pltpu.VMEM((4, D, FF), BF16),
            pltpu.VMEM((4, FF, D), BF16),
            pltpu.VMEM((8, 8, TOK), F32),
            pltpu.VMEM((8, 8, TOK), F32),
            pltpu.VMEM((2 * CAP, D), BF16),
            pltpu.VMEM((2, 4 * CAP, D), BF16),
            pltpu.VMEM((2, 4 * CAP, TOK), BF16),
            pltpu.VMEM((2, TOK, D), F32),
            pltpu.VMEM((4, TOK, D), BF16),
            pltpu.VMEM((4, TOK, D), BF16),
            pltpu.VMEM((3, TOK, D), BF16),
            dma((4,)), dma((3, 4)), dma((4,)), dma((4,)), dma((3,)), dma((3,)),
        ],
        compiler_params=pltpu.CompilerParams(
            vmem_limit_bytes=VMEM_BYTES, collective_id=1, has_side_effects=True
        ),
        name="tail",
    )(moe_all, ids, rw, *own, *gathered)


def local(
    tokens, attn_gain, w_query, w_key, w_value, w_out, prefix_keys, prefix_values,
    lengths, assignment, moe_gain, expert_ids, route_weights, w_gate, w_up, w_down,
):
    cos, sin = rope_tables()
    context, hidden, moe_all, ids, rw, wg, wu, wd = front(
        tokens[0], attn_gain[None], w_query, w_key, w_value, w_out, moe_gain[None], cos, sin,
        prefix_keys[0], prefix_values[0], assignment, lengths, expert_ids[0].T, route_weights[0].T, w_gate, w_up, w_down,
    )
    total, sums = tail(moe_all, ids, rw, (w_gate, w_up, w_down), (wg, wu, wd))
    expert_mix = (total + jnp.sum(sums.astype(F32), axis=0)).astype(BF16)
    return (context[None], hidden[None], expert_mix[None])


def solution(mesh):
    placed = (
        P("grp", "req", None), P(), P(), P(), P(), P(),
        P("grp", "req", None), P("grp", "req", None), P("grp", None), P("grp", None),
        P(), P("grp", "req", None), P("grp", "req", None),
        P("req", None, None), P("req", None, None), P("req", None, None),
    )
    return jax.shard_map(
        local,
        mesh=mesh,
        in_specs=placed,
        out_specs=(P("grp", "req", None), P("grp", "req", None), P("grp", "req", None)),
        check_vma=False,
    )
```

```python
import functools

import jax
import jax.numpy as jnp
import numpy as np
from jax import lax
from jax.experimental import pallas as pl
from jax.experimental.pallas import tpu as pltpu
from jax.sharding import PartitionSpec as P

HD = 64
CAP = 96
PREFIX = 8192
TOK = 256
D = 1024
FF = 512
NORM_EPS = 1e-06
ATTN_SCALE = 0.015625
RESIDUAL_SCALE = 0.22
ROPE_BASE = 10000.0
LOG2E = 1.4426950408889634
VMEM_BYTES = 60000 * 1024
BF16 = jnp.bfloat16
F32 = jnp.float32


def rope_tables():
    half = HD // 2
    freq = np.float32(ROPE_BASE) ** (-(np.arange(half, dtype=np.float32) * 2.0 / HD))
    pos = (PREFIX + np.arange(TOK)).astype(np.float32)
    angles = (pos[:, None] * freq.astype(np.float32)[None, :]).astype(np.float64)
    cos, sin = np.cos(angles), np.sin(angles)
    cos128 = np.concatenate([cos] * 4, axis=1).astype(np.float32)
    sin128 = np.concatenate([-sin, sin, -sin, sin], axis=1).astype(np.float32)
    return cos128, sin128


def vmem_specs(n):
    return [pl.BlockSpec(memory_space=pltpu.VMEM)] * n


def params():
    return pltpu.CompilerParams(vmem_limit_bytes=VMEM_BYTES)


MESH_ID = pl.DeviceIdType.MESH
KT = 512
ORDER = (0, 1, 3, 2)
HALF = 8
WIDE = ((256, 192), (256, 192), (128, 96))


def rem4(v):
    return lax.rem(v + 4, 4)


def front_kernel(
    tok_ref, again_ref, wq_ref, wk_ref, wv_ref, wo_ref, mgain_ref, cos_ref, sin_ref, pk_ref, pv_ref, assign_ref, lengths_ref,
    ids_in, rw_in, g_in, u_in, d_in,
    context_ref, hidden_ref, moe_all, ids_all, rw_all, g_all, u_all, d_all,
    kv8, kv_all, x_send, x_all, vt_ref, s_ref, q_st, m_st, acc_st, part_ref, ctx_all, moe_buf,
    kvs, kvr, xs, xr, cs, cr, ms, mr, ts, tr, ws, wr, vs, vr, zs, zr, own_sem,
):
    grp = lax.axis_index("grp")
    me = lax.axis_index("req")
    x, y, c = lax.div(me, 8), lax.rem(lax.div(me, 2), 4), lax.rem(me, 2)
    pos = 2 * x + c

    def remote(src, dst, send, recv, tx, ty, tc, tg=None):
        where = (grp if tg is None else tg, tx * 8 + ty * 2 + tc)
        return pltpu.make_async_remote_copy(
            src_ref=src, dst_ref=dst, send_sem=send, recv_sem=recv, device_id=where, device_id_type=MESH_ID
        )

    barrier = pltpu.get_barrier_semaphore()

    def greet(i, carry):
        pl.semaphore_signal(barrier, inc=1, device_id=(grp, lax.rem(me + i, 32)), device_id_type=MESH_ID)
        return carry

    lax.fori_loop(1, 32, greet, 0)
    for dz in (1, 2, 3):
        pl.semaphore_signal(barrier, inc=1, device_id=(rem4(grp + dz), me), device_id_type=MESH_ID)

    def own_copies():
        pairs = [(ids_in, ids_all.at[pos]), (rw_in, rw_all.at[pos])]
        return [pltpu.make_async_copy(a, b, own_sem.at[i]) for i, (a, b) in enumerate(pairs)]

    for cp in own_copies():
        cp.start()

    for pair in range(4):
        kr = pk_ref[:, 128 * pair : 128 * pair + 128]
        vr_ = pv_ref[:, 128 * pair : 128 * pair + 128]
        kv8[2 * pair] = jnp.concatenate([kr[:, 0:64], vr_[:, 0:64]], axis=1)
        kv8[2 * pair + 1] = jnp.concatenate([kr[:, 64:128], vr_[:, 64:128]], axis=1)
    mine = pl.ds(pl.multiple_of(me * TOK, TOK), TOK)
    kv_all[mine, :] = kv8[pos]
    pl.semaphore_wait(barrier, 34)

    def offset(half, j):
        t, u = lax.div(j, 4) - 2 * half, lax.rem(j, 4)
        side = 1 + 2 * lax.div(u, 2)
        if half == 0:
            dx = t * side
            return dx, (1 - t) * u + t * lax.rem(u, 2) * dx
        return (1 - t) * side + 2 * t, (1 - t) * (2 + lax.rem(u, 2) * (2 - side)) + t * u

    def kv_copy(half, j, tc):
        dx, dy = offset(half, j)
        tx, ty = lax.rem(x + dx, 4), lax.rem(y + dy, 4)
        return remote(kv8.at[2 * tx + tc], kv_all.at[mine, :], kvs.at[2 * j + tc], kvr.at[me], tx, ty, tc)

    def kv_each(half, what):
        def both(j, carry):
            for tc in (0, 1):
                what(kv_copy(half, j, tc))
            return carry

        if half == 0:
            what(remote(kv8.at[2 * x + 1 - c], kv_all.at[mine, :], kvs.at[0], kvr.at[me], x, y, 1 - c))
        lax.fori_loop(1 if half == 0 else HALF, HALF if half == 0 else 2 * HALF, both, 0)

    kv_each(0, lambda cp: cp.start())

    peers = [(0, 1)] + [(dx, dc) for dx in (1, 3, 2) for dc in (0, 1)]

    def peer(i):
        dx, dc = peers[i]
        return rem4(x + dx), lax.rem(c + dc, 2)

    def table_copies(i):
        tx, tc = peer(i)
        return (
            remote(ids_in, ids_all.at[pos], ts.at[0, i], tr.at[0, i], tx, y, tc),
            remote(rw_in, rw_all.at[pos], ts.at[1, i], tr.at[1, i], tx, y, tc),
        )

    for i in range(7):
        for cp in table_copies(i):
            cp.start()

    stacks = ((g_in, g_all), (u_in, u_all), (d_in, d_all))

    def quarter_rows(t, z=None):
        straight, quarter = WIDE[t]
        return pl.ds(pl.multiple_of(straight + (grp if z is None else z) * quarter, 16), quarter)

    def weight_copies(dy, part, only=(0, 1, 2)):
        out = []
        for t in only:
            src, dst = stacks[t]
            rows = quarter_rows(t) if part else pl.ds(0, WIDE[t][0])
            sems = (vs, vr) if part else (ws, wr)
            out.append(
                remote(src.at[0, rows, :], dst.at[3 - dy, rows, :], sems[0].at[dy - 1, t], sems[1].at[dy - 1, t],
                       x, rem4(y + dy), c)
            )
        return out

    def column_copies(t):
        dst, rows = stacks[t][1], quarter_rows(t)
        return [
            remote(dst.at[slot, rows, :], dst.at[slot, rows, :], zs.at[i, slot, t], zr.at[i, slot, t],
                   x, y, c, rem4(grp + dz))
            for slot in range(3)
            for i, dz in enumerate((1, 3))
        ]

    def beyond_copies(t):
        dst, out = stacks[t][1], []
        for slot in range(3):
            step = 1 - 2 * ((slot + t) % 2)
            rows = quarter_rows(t, rem4(grp - step))
            out.append(
                remote(dst.at[slot, rows, :], dst.at[slot, rows, :], zs.at[2, slot, t], zr.at[2, slot, t],
                       x, y, c, rem4(grp + step))
            )
        return out

    def weights_start(part, only):
        for dy in (1, 3, 2):
            for cp in weight_copies(dy, part, only):
                cp.start()

    def column_start(t):
        for dy in (1, 3, 2):
            for cp in weight_copies(dy, 1, (t,)):
                cp.wait_recv()
        for cp in column_copies(t):
            cp.start()

    def beyond_start(t):
        for cp in column_copies(t):
            cp.wait_recv()
        for cp in beyond_copies(t):
            cp.start()

    weights_start(1, (0,))

    rows = tok_ref[...].astype(F32)
    mean_square = jnp.mean(rows * rows, axis=-1, keepdims=True)
    normed = (rows * lax.rsqrt(mean_square + NORM_EPS) * again_ref[...]).astype(BF16)
    cos, sin = cos_ref[...], sin_ref[...]
    low = (lax.broadcasted_iota(jnp.int32, (TOK, 128), 1) & 32) == 0

    def rotate(part):
        other = jnp.where(low, pltpu.roll(part, 96, 1), pltpu.roll(part, 32, 1))
        return (part * cos + other * sin).astype(BF16)

    q = jnp.dot(normed, wq_ref[...], preferred_element_type=F32)
    k = jnp.dot(normed, wk_ref[...], preferred_element_type=F32)
    v = jnp.dot(normed, wv_ref[...], preferred_element_type=F32).astype(BF16)
    for h in range(8):
        x_send[h, :, 0:128] = rotate(q[:, 128 * h : 128 * h + 128])
    for pair in range(4):
        kr = rotate(k[:, 128 * pair : 128 * pair + 128])
        vr_ = v[:, 128 * pair : 128 * pair + 128]
        x_send[2 * pair, :, 128:256] = jnp.concatenate([kr[:, 0:64], vr_[:, 0:64]], axis=1)
        x_send[2 * pair + 1, :, 128:256] = jnp.concatenate([kr[:, 64:128], vr_[:, 64:128]], axis=1)
    x_all[pos] = x_send[pos]

    def x_copy(i):
        tx, tc = peer(i)
        return remote(x_send.at[2 * tx + tc], x_all.at[pos], xs.at[i], xr.at[i], tx, y, tc)

    for i in range(7):
        x_copy(i).start()
    kv_each(1, lambda cp: cp.start())
    vt_ref[64:80, :] = jnp.ones((16, PREFIX), BF16)

    def keys_of(half, j):
        dx, dy = offset(half, j)
        chip = lax.rem(x + 4 - dx, 4) * 4 + lax.rem(y + 4 - dy, 4)
        return chip, pl.ds(pl.multiple_of(chip * KT, KT), KT)

    def arrive(src):
        spot = pl.ds(pl.multiple_of(src * TOK, TOK), TOK)
        remote(kv8.at[0], kv_all.at[spot, :], kvs.at[0], kvr.at[src], x, y, 1 - c).wait_recv()

    def score(fresh, half, j, q2):
        chip, ds = keys_of(half, j)
        block = kv_all[ds, :]
        if fresh:
            vt_ref[0:64, ds] = block.T[64:128]
        return jnp.dot(block, q2, preferred_element_type=F32)

    def suffix_len(member):
        lane = lax.broadcasted_iota(jnp.int32, (1, 32), 1)
        request = jnp.sum(jnp.where(lane == member, assign_ref[...].astype(F32), 0.0), axis=1, keepdims=True)
        return jnp.sum(
            jnp.where(lane.astype(F32) == request, lengths_ref[...].astype(F32), 0.0), axis=1, keepdims=True
        )

    def begin(kth):
        tx = rem4(x + ORDER[kth])
        back = (4 - ORDER[kth]) % 4
        for i, (dx, dc) in enumerate(peers):
            if dx == back:
                x_copy(i).wait_recv()
        for j in range(2):
            blk = x_all[2 * tx + j]
            qt = (blk[:, 0:128].astype(F32) * ATTN_SCALE).astype(BF16).T
            q2 = jnp.concatenate([qt[0:64], qt[64:128]], axis=1)
            q2 = jnp.concatenate([q2, jnp.zeros((64, 512), BF16)], axis=0)
            skv = blk[:, 128:256]
            s = jnp.dot(skv, q2, preferred_element_type=F32)
            srow = lax.broadcasted_iota(jnp.int32, (TOK, 512), 0)
            tcol = lax.broadcasted_iota(jnp.int32, (TOK, 512), 1) & 255
            visible = (srow <= tcol) & (srow.astype(F32) < suffix_len(tx * 8 + y * 2 + j))
            s = jnp.where(visible, s * LOG2E, -jnp.inf)
            m = jnp.max(s, axis=0, keepdims=True)
            p = jnp.exp2(s - m)
            l = jnp.sum(p, axis=0, keepdims=True)
            acc = jnp.dot(skv.T[64:128], p.astype(BF16), preferred_element_type=F32)
            cols = slice(512 * j, 512 * (j + 1))
            q_st[kth, :, cols] = q2
            m_st[kth, :, cols] = m
            acc_st[kth, 0:64, cols] = acc
            acc_st[kth, 64:80, cols] = jnp.broadcast_to(l, (16, 512))

    def attend(kth, half, fresh):
        q2 = q_st[kth]
        lo, hi = half * HALF, half * HALF + HALF
        if fresh and half == 0:
            arrive(2 * (4 * x + y) + 1 - c)
        elif fresh:
            chip, ds = keys_of(half, jnp.int32(lo))
            arrive(2 * chip)
            arrive(2 * chip + 1)
        s_ref[0] = score(fresh, half, jnp.int32(lo), q2)

        def step(i, carry):
            m, acc = carry
            for u in range(2):
                kk = lo + 2 * i + u
                nxt = jnp.minimum(kk + 1, hi - 1)
                if fresh:

                    @pl.when(kk + 1 < hi)
                    def _():
                        chip, ds = keys_of(half, nxt)
                        arrive(2 * chip)
                        arrive(2 * chip + 1)

                s = s_ref[u]
                s_ref[1 - u] = score(fresh, half, nxt, q2)
                s = s * LOG2E
                mn = jnp.maximum(m, jnp.max(s, axis=0, keepdims=True))
                p = jnp.exp2(s - mn).astype(BF16)
                chip, ds = keys_of(half, kk)
                acc = acc * jnp.exp2(m - mn) + jnp.dot(vt_ref[:, ds], p, preferred_element_type=F32)
                m = mn
            return m, acc

        m, acc = lax.fori_loop(0, HALF // 2, step, (m_st[kth], acc_st[kth]))
        if half == 0:
            m_st[kth] = m
            acc_st[kth] = acc
            return
        tx = rem4(x + ORDER[kth])
        out = acc[0:64] / acc[64:65]
        for j in range(2):
            ot = out[:, 512 * j : 512 * (j + 1)].T.astype(BF16)
            part_ref[2 * tx + j] = jnp.concatenate([ot[0:256], ot[256:512]], axis=1)

    def ctx_copy(i):
        tx, tc = peer(i)
        return remote(part_ref.at[2 * tx + tc], ctx_all.at[pos], cs.at[i], cr.at[i], tx, y, tc)

    for kth in range(4):
        if kth == 2:
            column_start(0)
            weights_start(1, (1,))
        if kth == 3:
            weights_start(1, (2,))
        begin(kth)
        attend(kth, 0, kth == 0)
    for kth in (3, 1, 2, 0):
        if kth == 1:
            column_start(1)
            beyond_start(0)
            weights_start(0, (0,))
        if kth == 2:
            weights_start(0, (1,))
        if kth == 0:
            column_start(2)
            beyond_start(1)
            weights_start(0, (2,))
        attend(kth, 1, kth == 3)
        if kth == 0:
            ctx_all[pos] = part_ref[pos]
        for i, (dx, dc) in enumerate(peers):
            if dx == ORDER[kth]:
                ctx_copy(i).start()

    for i in range(7):
        ctx_copy(i).wait_recv()
    ctx = jnp.concatenate([ctx_all[h] for h in range(8)], axis=1)
    context_ref[...] = ctx
    projected = jnp.dot(ctx, wo_ref[...], preferred_element_type=F32)
    hidden = (tok_ref[...].astype(F32) + RESIDUAL_SCALE * projected).astype(BF16)
    hidden_ref[...] = hidden
    wide = hidden.astype(F32)
    mean_square = jnp.mean(wide * wide, axis=-1, keepdims=True)
    moe_buf[...] = (wide * lax.rsqrt(mean_square + NORM_EPS) * mgain_ref[...]).astype(BF16)

    def moe_copy(i, dx):
        return remote(moe_buf, moe_all.at[pos], ms.at[i], mr.at[i], rem4(x + dx), y, c)

    def onward_copy(i):
        step = 1 - 2 * i
        rows = pl.ds(TOK // 2 * i, TOK // 2)
        block = moe_all.at[2 * rem4(x - step) + c, rows, :]
        return remote(block, block, ms.at[2 + i], mr.at[2 + i], rem4(x + step), y, c)

    def relay_copy(i, spot, src):
        return remote(src, moe_all.at[spot], ms.at[4 + i], mr.at[4 + i], x, y, 1 - c)

    keep = pltpu.make_async_copy(moe_buf, moe_all.at[pos], own_sem.at[2])
    for i, dx in enumerate((1, 3)):
        moe_copy(i, dx).start()
    relays = [relay_copy(3, pos, moe_buf)]
    relays[0].start()
    keep.start()
    beyond_start(2)
    for i, dx in enumerate((1, 3)):
        moe_copy(i, dx).wait_recv()
        onward_copy(i).start()
        spot = 2 * rem4(x - dx) + c
        relays.append(relay_copy(i, spot, moe_all.at[spot]))
        relays[-1].start()
    for i in range(2):
        onward_copy(i).wait_recv()
    spot = 2 * rem4(x + 2) + c
    relays.append(relay_copy(2, spot, moe_all.at[spot]))
    relays[-1].start()

    keep.wait()
    for cp in own_copies():
        cp.wait()
    for i, dx in enumerate((1, 3)):
        moe_copy(i, dx).wait_send()
        onward_copy(i).wait_send()
    for cp in relays:
        cp.wait()
    for i in range(7):
        x_copy(i).wait_send()
        ctx_copy(i).wait_send()
        for cp in table_copies(i):
            cp.wait()
    for half in (0, 1):
        kv_each(half, lambda cp: cp.wait_send())
    for dy in (1, 3, 2):
        for cp in weight_copies(dy, 1):
            cp.wait_send()
        for cp in weight_copies(dy, 0):
            cp.wait()
    for t in range(3):
        for cp in column_copies(t):
            cp.wait_send()
        for cp in beyond_copies(t):
            cp.wait()


def front(*args):
    anywhere = pl.BlockSpec(memory_space=pl.ANY)
    dma = pltpu.SemaphoreType.DMA
    shape = jax.ShapeDtypeStruct
    return pl.pallas_call(
        front_kernel,
        out_shape=(
            shape((TOK, D), BF16), shape((TOK, D), BF16), shape((8, TOK, D), BF16),
            shape((8, 8, TOK), jnp.int32), shape((8, 8, TOK), F32),
            shape((3, D, FF), BF16), shape((3, D, FF), BF16), shape((3, FF, D), BF16),
        ),
        in_specs=vmem_specs(13) + [anywhere] * 5,
        out_specs=tuple(vmem_specs(2) + [anywhere] * 6),
        scratch_shapes=[
            pltpu.VMEM((8, TOK, 128), BF16),
            pltpu.VMEM((PREFIX, 128), BF16),
            pltpu.VMEM((8, TOK, 256), BF16),
            pltpu.VMEM((8, TOK, 256), BF16),
            pltpu.VMEM((80, PREFIX), BF16),
            pltpu.VMEM((2, KT, 1024), F32),
            pltpu.VMEM((4, 128, 1024), BF16),
            pltpu.VMEM((4, 1, 1024), F32),
            pltpu.VMEM((4, 80, 1024), F32),
            pltpu.VMEM((8, TOK, 128), BF16),
            pltpu.VMEM((8, TOK, 128), BF16),
            pltpu.VMEM((TOK, D), BF16),
            dma((32,)), dma((32,)), dma((7,)), dma((7,)), dma((7,)), dma((7,)), dma((8,)), dma((8,)),
            dma((2, 7)), dma((2, 7)), dma((3, 3)), dma((3, 3)), dma((3, 3)), dma((3, 3)),
            dma((3, 3, 3)), dma((3, 3, 3)), dma((3,)),
        ],
        compiler_params=pltpu.CompilerParams(
            vmem_limit_bytes=VMEM_BYTES, collective_id=0, has_side_effects=True
        ),
        name="front",
    )(*args)


PHASES = (2, 1, 3, 0)


def tail_kernel(
    moe_all, ids_ref, rw_ref, g_in, u_in, d_in, g_all, u_all, d_all, mix_ref,
    x_v, g_v, u_v, d_v, rank_ref, wt_ref, rows_ref, eo_ref, pw_ref, keep_ref,
    pair_send, pair_recv, out_send, out_recv, xsem, wsem, ps, pr, os, orr,
):
    grp = lax.axis_index("grp")
    me = lax.axis_index("req")
    x, y, c = lax.div(me, 8), lax.rem(lax.div(me, 2), 4), lax.rem(me, 2)

    def remote(src, dst, send, recv, tx, tc):
        return pltpu.make_async_remote_copy(
            src_ref=src, dst_ref=dst, send_sem=send, recv_sem=recv,
            device_id=(grp, tx * 8 + y * 2 + tc), device_id_type=MESH_ID,
        )

    barrier = pltpu.get_barrier_semaphore()
    for tx, tc in [(x, 1 - c)] + [(rem4(x + dx), c) for dx in (1, 2, 3)]:
        pl.semaphore_signal(barrier, inc=1, device_id=(grp, tx * 8 + y * 2 + tc), device_id_type=MESH_ID)

    def two(k):
        return pl.ds(2 * rem4(x + PHASES[k]), 2)

    def load_rows(k):
        return pltpu.make_async_copy(moe_all.at[two(k)], x_v.at[k], xsem.at[k])

    def load_weights(e, own=False):
        sources = (g_in, u_in, d_in) if own else (g_all, u_all, d_all)
        return [
            pltpu.make_async_copy(src.at[0 if own else e], dst.at[e], wsem.at[t, e])
            for t, (src, dst) in enumerate(zip(sources, (g_v, u_v, d_v)))
        ]

    load_rows(0).start()
    for e in range(4):
        for cp in load_weights(e, e == 3):
            cp.start()
        if e < 3:
            load_rows(e + 1).start()

    tri = (
        lax.broadcasted_iota(jnp.int32, (TOK, TOK), 0) < lax.broadcasted_iota(jnp.int32, (TOK, TOK), 1)
    ).astype(BF16)
    for b in range(8):
        masks, weights = [], []
        for e in range(4):
            hits = ids_ref[b] == x * 8 + rem4(y + 1 + e) * 2 + c
            masks.append(jnp.max(hits.astype(F32), axis=0, keepdims=True))
            weights.append(jnp.sum(jnp.where(hits, rw_ref[b], 0.0), axis=0, keepdims=True))
        mask = jnp.concatenate(masks + [jnp.zeros((12, TOK), F32)], axis=0)
        rank = jnp.dot(mask.astype(BF16), tri, preferred_element_type=F32)
        rank_ref[b] = jnp.where(mask > 0, rank, -1.0)[0:8]
        wt_ref[b] = jnp.concatenate(weights + [jnp.zeros((4, TOK), F32)], axis=0)
    slot = lax.broadcasted_iota(jnp.int32, (CAP, TOK), 0).astype(F32)
    pl.semaphore_wait(barrier, 4)

    def pair_copy(k):
        return remote(pair_send.at[k], pair_recv.at[k], ps.at[k], pr.at[k], x, 1 - c)

    def out_copy(k):
        return remote(out_send.at[k], out_recv.at[k], os.at[k], orr.at[k], rem4(x + PHASES[k]), c)

    def finish(k):
        pair_copy(k).wait_recv()
        total = keep_ref[k % 2] + pair_recv[k].astype(F32)
        if k < 3:
            out_send[k] = total.astype(BF16)
            out_copy(k).start()
        return total

    for k in range(4):
        base = 2 * rem4(x + PHASES[k])
        load_rows(k).wait()

        def expert(e, carry):
            if k == 0:
                for src, dst, t in ((g_in, g_v, 0), (u_in, u_v, 1), (d_in, d_v, 2)):
                    pltpu.make_async_copy(src.at[0], dst.at[e], wsem.at[t, e]).wait()
            here = pl.ds(pl.multiple_of(e * CAP, CAP), CAP)
            for j in range(2):
                chosen = slot == rank_ref[base + j, pl.ds(e, 1), :]
                rows_ref[j * CAP : (j + 1) * CAP] = jnp.dot(
                    chosen.astype(BF16), x_v[k, j], preferred_element_type=F32
                ).astype(BF16)
                pw_ref[j, here] = jnp.where(chosen, wt_ref[base + j, pl.ds(e, 1), :], 0.0).astype(BF16)
            rows = rows_ref[...]
            gate = jnp.dot(rows, g_v[e], preferred_element_type=F32)
            up = jnp.dot(rows, u_v[e], preferred_element_type=F32)
            act = (jax.nn.silu(gate) * up).astype(BF16)
            out = jnp.dot(act, d_v[e], preferred_element_type=F32).astype(BF16)
            for j in range(2):
                eo_ref[j, here] = out[j * CAP : (j + 1) * CAP]
            if k > 0:

                @pl.when(e == 0)
                def _():
                    finish(k - 1)

            return carry

        lax.fori_loop(0, 4, expert, 0)

        def combine(j):
            return lax.dot_general(pw_ref[j], eo_ref[j], (((0,), (0,)), ((), ())), preferred_element_type=F32)

        pair_send[k] = combine(1 - c).astype(BF16)
        pair_copy(k).start()
        keep_ref[k % 2] = combine(c)
    total = finish(3)
    for k in range(3):
        out_copy(k).wait_recv()
        total = total + out_recv[k].astype(F32)
    mix_ref[...] = total.astype(BF16)
    for k in range(4):
        pair_copy(k).wait_send()
    for k in range(3):
        out_copy(k).wait_send()


def tail(moe_all, ids, rw, own, gathered):
    anywhere = pl.BlockSpec(memory_space=pl.ANY)
    dma = pltpu.SemaphoreType.DMA
    return pl.pallas_call(
        tail_kernel,
        out_shape=jax.ShapeDtypeStruct((TOK, D), BF16),
        in_specs=[anywhere] + vmem_specs(2) + [anywhere] * 6,
        out_specs=vmem_specs(1)[0],
        scratch_shapes=[
            pltpu.VMEM((4, 2, TOK, D), BF16),
            pltpu.VMEM((4, D, FF), BF16),
            pltpu.VMEM((4, D, FF), BF16),
            pltpu.VMEM((4, FF, D), BF16),
            pltpu.VMEM((8, 8, TOK), F32),
            pltpu.VMEM((8, 8, TOK), F32),
            pltpu.VMEM((2 * CAP, D), BF16),
            pltpu.VMEM((2, 4 * CAP, D), BF16),
            pltpu.VMEM((2, 4 * CAP, TOK), BF16),
            pltpu.VMEM((2, TOK, D), F32),
            pltpu.VMEM((4, TOK, D), BF16),
            pltpu.VMEM((4, TOK, D), BF16),
            pltpu.VMEM((3, TOK, D), BF16),
            pltpu.VMEM((3, TOK, D), BF16),
            dma((4,)), dma((3, 4)), dma((4,)), dma((4,)), dma((3,)), dma((3,)),
        ],
        compiler_params=pltpu.CompilerParams(
            vmem_limit_bytes=VMEM_BYTES, collective_id=1, has_side_effects=True
        ),
        name="tail",
    )(moe_all, ids, rw, *own, *gathered)


def local(
    tokens, attn_gain, w_query, w_key, w_value, w_out, prefix_keys, prefix_values,
    lengths, assignment, moe_gain, expert_ids, route_weights, w_gate, w_up, w_down,
):
    cos, sin = rope_tables()
    context, hidden, moe_all, ids, rw, wg, wu, wd = front(
        tokens[0], attn_gain[None], w_query, w_key, w_value, w_out, moe_gain[None], cos, sin,
        prefix_keys[0], prefix_values[0], assignment, lengths, expert_ids[0].T, route_weights[0].T, w_gate, w_up, w_down,
    )
    expert_mix = tail(moe_all, ids, rw, (w_gate, w_up, w_down), (wg, wu, wd))
    return (context[None], hidden[None], expert_mix[None])


def solution(mesh):
    placed = (
        P("grp", "req", None), P(), P(), P(), P(), P(),
        P("grp", "req", None), P("grp", "req", None), P("grp", None), P("grp", None),
        P(), P("grp", "req", None), P("grp", "req", None),
        P("req", None, None), P("req", None, None), P("req", None, None),
    )
    return jax.shard_map(
        local,
        mesh=mesh,
        in_specs=placed,
        out_specs=(P("grp", "req", None), P("grp", "req", None), P("grp", "req", None)),
        check_vma=False,
    )
```
